32 devices in a mesh: dp: 4 (over x, core), fsdp: 8 (over z, y).
Axes of the slice: x: 2, y: 2, z: 4, core: 2. Of those that a mesh axis runs over, the one named last changes fastest.
Arguments:
- inputs: bfloat16 [8192, 2048], P(('dp', 'fsdp')), may hold values from -18 to 18
- kv_input: bfloat16 [8192, 2048], P(('dp', 'fsdp')), may hold values from -6 to 6
- segment_ids: int32 [8192], P(('dp', 'fsdp')), may hold values from 0 to 15, never falling along the last dimension, each value on 1 to 1024 neighbouring positions
- valid_mask: int32 [8192], P(('dp', 'fsdp')), may hold values from 0 to 1, as said below
- w_query: bfloat16 [2048, 2048], P(('dp', 'fsdp')), may hold values from -0.125 to 0.125
- w_key: bfloat16 [2048, 2048], P(('dp', 'fsdp')), may hold values from -0.125 to 0.125
- w_value: bfloat16 [2048, 2048], P(('dp', 'fsdp')), may hold values from -0.125 to 0.125
- w_out: bfloat16 [2048, 2048], P(('dp', 'fsdp')), may hold values from -1 to 1
- w_gate: bfloat16 [2048, 5504], P(('dp', 'fsdp')), may hold values from -0.125 to 0.125
- w_up: bfloat16 [2048, 5504], P(('dp', 'fsdp')), may hold values from -0.125 to 0.125
- w_down: bfloat16 [5504, 2048], P(('dp', 'fsdp')), may hold values from -0.078125 to 0.078125
- gain_attn: bfloat16 [2048], P(('dp', 'fsdp')), may hold values from 0.099609375 to 1.8984375
- gain_ffn: bfloat16 [2048], P(('dp', 'fsdp')), may hold values from 0.099609375 to 1.8984375
- cotangent: bfloat16 [8192, 2048], P(('dp', 'fsdp')), may hold values from -6 to 6
Outputs:
- output: bfloat16 [8192, 2048], P(('dp', 'fsdp'))
- grad_inputs: float32 [8192, 2048], P(('dp', 'fsdp'))
- grad_kv_input: float32 [8192, 2048], P(('dp', 'fsdp'))
- grad_w_query: float32 [2048, 2048], P(('dp', 'fsdp'))
- grad_w_key: float32 [2048, 2048], P(('dp', 'fsdp'))
- grad_w_value: float32 [2048, 2048], P(('dp', 'fsdp'))
- grad_w_out: float32 [2048, 2048], P(('dp', 'fsdp'))
- grad_w_gate: float32 [2048, 5504], P(('dp', 'fsdp'))
- grad_w_up: float32 [2048, 5504], P(('dp', 'fsdp'))
- grad_w_down: float32 [5504, 2048], P(('dp', 'fsdp'))
- grad_gain_attn: float32 [2048], P(('dp', 'fsdp'))
- grad_gain_ffn: float32 [2048], P(('dp', 'fsdp'))
- rms_in: float32 [], replicated
- rms_mid: float32 [], replicated
- rms_out: float32 [], replicated
The draws below stay inside these ranges and needn't reach their ends.
Inputs may be any that keep to these rules, and one draw needn't show every extreme that they name: `valid_mask`: 1 for real tokens; padding fills the last 0 to 256 tokens of each block of 2048. `segment_ids`: never falling along the tokens; each id covers 1 to 1024 consecutive tokens.
All inputs are finite; a program needn't handle non-finite values.
Results may differ from the reference program's by a relative error of at most 0.017.
Values may be sent and summed in bfloat16 or wider, within the bound.
No kernel may reach another device: no remote copies, remote signals or barrier semaphores. Data moves between devices by JAX's collectives and lax.ppermute only.
A program may use at most 576 MiB of HBM per device.

```python
import math
import jax
import jax.numpy as jnp
import numpy as np
from jax import lax

D = 2048
HEADS = 16
HEAD_DIM = 128
FF = 5504
TOKENS = 8192
LENGTH = 2048


def draw_inputs(key, part):
    rows = jnp.arange(TOKENS, dtype=jnp.float32)
    ramp = 1.0 + 2.0 * rows / (TOKENS - 1)
    base = jnp.clip(jax.random.normal(key, (TOKENS, D), jnp.float32), -6.0, 6.0)
    return (base * ramp[:, None]).astype(jnp.bfloat16)


def draw_valid_mask(key, part):
    sequences = TOKENS // LENGTH
    padding = jax.random.randint(key, (sequences,), 0, LENGTH // 8 + 1)
    padding = padding.at[0].set(LENGTH // 8)
    position = jnp.arange(LENGTH, dtype=jnp.int32)
    live = position[None, :] < (LENGTH - padding)[:, None]
    return live.astype(jnp.int32).reshape(TOKENS)


def block_levels(key, dims, pieces, smallest, high):
    gain, own = 1.0, jax.random.fold_in(key, 6)
    for axis_at, parts in pieces:
        steps = jnp.exp(jax.random.uniform(jax.random.fold_in(own, axis_at), (parts,), jnp.float32, smallest / len(pieces), high / len(pieces)))
        gain = gain * jnp.repeat(steps, dims[axis_at] // parts).reshape([-1 if axis == axis_at else 1 for axis in range(len(dims))])
    return gain


def profile(amount, total, most, slope):
    weights = [(1 << 20) // math.isqrt(rank ** slope) + 1 for rank in range(2, amount + 1)]
    spare, holding = total - most - (amount - 1), [1] * (amount - 1)
    while spare > 0:
        free = [i for i in range(amount - 1) if holding[i] < most]
        whole, left = sum([weights[i] for i in free]), spare
        for i in free:
            addition = min(most - holding[i], max(1, left * weights[i] // whole), spare)
            holding[i] = holding[i] + addition
            spare = spare - addition
    return np.array([most] + holding)


def uneven_parts(own_key, amount, total, limit, slope):
    if amount == 2:
        one = jax.random.randint(own_key, (), max(1, total - limit), min(limit, total - 1) + 1)
        return jnp.stack([one, total - one])
    tallies = jnp.asarray(profile(amount, total, limit, slope), jnp.int32)
    couples = (amount - 1) // 2
    giver, taker = tallies[1:1 + 2 * couples:2], tallies[2:2 + 2 * couples:2]
    slack = jnp.minimum(giver - 1, limit - taker)
    passed = jax.random.randint(jax.random.fold_in(own_key, 1), (couples,), 0, 1 << 20) % (slack + 1)
    tallies = tallies.at[1:1 + 2 * couples:2].set(giver - passed).at[2:2 + 2 * couples:2].set(taker + passed)
    return tallies[jax.random.permutation(jax.random.fold_in(own_key, 2), amount)]


def gaussian(key, dims, width, reach, pieces=(), kind=jnp.bfloat16):
    entries = jax.random.normal(key, dims, jnp.float32) * width
    if len(pieces) > 0:
        entries = block_levels(key, dims, pieces, -0.22, 0.18) * entries
    return jnp.clip(entries, min=-reach, max=reach).astype(kind)


def setup_inputs(seed: int = 0) -> dict:
    splits = jax.random.split(jax.random.key(seed), 15)
    return {
        "inputs": draw_inputs(jax.random.fold_in(splits[14], 71), 0),
        "kv_input": gaussian(splits[1], (TOKENS, D), 1.0, 6.0, ((0, 32),)),
        "segment_ids": jnp.searchsorted(jnp.cumsum(uneven_parts(splits[2], TOKENS // (LENGTH // 4), TOKENS, LENGTH // 2, 1)), jnp.arange(TOKENS), side="right").astype(jnp.int32),
        "valid_mask": draw_valid_mask(jax.random.fold_in(splits[14], 71), 0),
        "w_query": gaussian(splits[4], (D, D), D ** -0.5, 0.125, ((0, 32),)),
        "w_key": gaussian(splits[5], (D, D), D ** -0.5, 0.125, ((0, 32),)),
        "w_value": gaussian(splits[6], (D, D), D ** -0.5, 0.125, ((0, 32),)),
        "w_out": gaussian(splits[7], (D, D), (D // 64) ** -0.5, 1.0, ((0, 32),)),
        "w_gate": gaussian(splits[8], (D, FF), D ** -0.5, 0.125, ((0, 32),)),
        "w_up": gaussian(splits[9], (D, FF), D ** -0.5, 0.125, ((0, 32),)),
        "w_down": gaussian(splits[10], (FF, D), FF ** -0.5, 0.078125, ((0, 32),)),
        "gain_attn": jnp.clip(1.0 + 0.18 * jax.random.normal(splits[11], (D,), jnp.float32), 0.099609375, 1.8984375).astype(jnp.bfloat16),
        "gain_ffn": jnp.clip(1.0 + 0.18 * jax.random.normal(splits[12], (D,), jnp.float32), 0.099609375, 1.8984375).astype(jnp.bfloat16),
        "cotangent": gaussian(splits[13], (TOKENS, D), 1.0, 6.0, ((0, 32),)),
    }


@jax.custom_vjp
def low(v):
    return lax.optimization_barrier(v.astype(jnp.bfloat16)).astype(jnp.float32)

@jax.custom_vjp
def low_back(v):
    return v

def low_keep(v):
    return (low(v), None)

def low_pass(kept, grad):
    return (grad,)

def back_keep(v):
    return (v, None)

def back_low(kept, grad):
    return (low(grad),)
low.defvjp(low_keep, low_pass)
low_back.defvjp(back_keep, back_low)
EPSILON = 1e-06

def product(left_side, right_side):
    return jnp.dot(left_side, right_side, precision=lax.Precision.HIGHEST, preferred_element_type=jnp.float32)

def rms_scaled(values, gains):
    factor = lax.rsqrt(lax.optimization_barrier(jnp.mean(values * values, axis=-1, keepdims=True)) + EPSILON)
    return values * factor * gains

def attention(queries, key_proj, value_proj, segment_ids, valid_mask):
    sequences = TOKENS // LENGTH
    query_rows = min(512, LENGTH)
    per_sequence = LENGTH // query_rows
    score_scale = 1.0 / math.sqrt(HEAD_DIM)
    query_all = queries.reshape(sequences, LENGTH, HEADS, HEAD_DIM)
    key_all = key_proj.reshape(sequences, LENGTH, HEADS, HEAD_DIM)
    value_all = value_proj.reshape(sequences, LENGTH, HEADS, HEAD_DIM)
    segment_all = segment_ids.reshape(sequences, LENGTH)
    valid_all = valid_mask.reshape(sequences, LENGTH)
    position = jnp.arange(LENGTH, dtype=jnp.int32)

    def one_block(block_index):
        sequence = block_index // per_sequence
        first_row = block_index % per_sequence * query_rows
        query_seq = lax.dynamic_index_in_dim(query_all, sequence, 0, keepdims=False)
        query_block = lax.dynamic_slice_in_dim(query_seq, first_row, query_rows, 0)
        key_seq = lax.dynamic_index_in_dim(key_all, sequence, 0, keepdims=False)
        value_seq = lax.dynamic_index_in_dim(value_all, sequence, 0, keepdims=False)
        segment_seq = lax.dynamic_index_in_dim(segment_all, sequence, 0, keepdims=False)
        valid_seq = lax.dynamic_index_in_dim(valid_all, sequence, 0, keepdims=False)
        segment_query = lax.dynamic_slice_in_dim(segment_seq, first_row, query_rows, 0)
        query_pos = first_row + jnp.arange(query_rows, dtype=jnp.int32)
        allowed = (segment_query[:, None] == segment_seq[None, :]) & (position[None, :] <= query_pos[:, None])
        allowed = allowed & ((valid_seq[None, :] == 1) | (position[None, :] == query_pos[:, None]))
        scores = low_back(jnp.einsum('qhd,khd->hqk', query_block, key_seq, precision=lax.Precision.HIGHEST) * score_scale)
        weights = jnp.where(allowed[None, :, :], jnp.exp(scores), 0.0)
        totals = lax.optimization_barrier(jnp.sum(weights, axis=-1))
        unnorm = low_back(jnp.einsum('hqk,khd->qhd', low(weights), value_seq, precision=lax.Precision.HIGHEST))
        return unnorm / jnp.transpose(totals)[:, :, None]
    blocks = lax.map(jax.checkpoint(one_block), jnp.arange(sequences * per_sequence, dtype=jnp.int32))
    return blocks.reshape(TOKENS, HEADS * HEAD_DIM)

def reference(inputs, kv_input, segment_ids, valid_mask, w_query, w_key, w_value, w_out, w_gate, w_up, w_down, gain_attn, gain_ffn, cotangent):

    def forward(stream, shared, query_w, key_w, value_w, out_w, gate_w, up_w, down_w, attn_gain, ffn_gain):
        normed1 = low(rms_scaled(stream, attn_gain))
        queries = low(low_back(product(normed1, query_w)))
        key_proj = low(low_back(product(shared, key_w)))
        value_proj = low(low_back(product(shared, value_w)))
        attended = low(attention(queries, key_proj, value_proj, segment_ids, valid_mask))
        middle = stream + low_back(product(attended, out_w))
        normed2 = low(rms_scaled(middle, ffn_gain))
        gate_proj = low_back(product(normed2, gate_w))
        up_proj = low_back(product(normed2, up_w))
        activation = low(jax.nn.silu(gate_proj) * up_proj)
        result = middle + low_back(product(activation, down_w))
        return (result, middle)
    stream = inputs.astype(jnp.float32)
    result, pullback, middle = jax.vjp(forward, stream, kv_input.astype(jnp.float32), w_query.astype(jnp.float32), w_key.astype(jnp.float32), w_value.astype(jnp.float32), w_out.astype(jnp.float32), w_gate.astype(jnp.float32), w_up.astype(jnp.float32), w_down.astype(jnp.float32), gain_attn.astype(jnp.float32), gain_ffn.astype(jnp.float32), has_aux=True)
    grads = pullback(cotangent.astype(jnp.float32))
    valid_float = valid_mask.astype(jnp.float32)
    count = jnp.sum(valid_float)

    def root_mean(values):
        return jnp.sqrt(jnp.sum(valid_float * lax.optimization_barrier(jnp.sum(values * values, axis=-1))) / (count * D))
    return (result.astype(jnp.bfloat16), grads[0], grads[1], grads[2], grads[3], grads[4], grads[5], grads[6], grads[7], grads[8], grads[9], grads[10], root_mean(stream), root_mean(middle), root_mean(result))
```

```python
import functools
import math

import jax
import jax.numpy as jnp
from jax import lax
from jax.experimental import pallas as pl
from jax.experimental.pallas import tpu as pltpu
from jax.sharding import Mesh
from jax.sharding import PartitionSpec as P

HEAD_DIM = 128
SEQ_LEN = 4096
EPSILON = 1e-06
ALL = ("x", "core", "z", "y")
GROUP = ("x", "core", "y")
F32 = jnp.float32
BF16 = jnp.bfloat16


def dot_nn(a, b):
    return lax.dot_general(a, b, (((1,), (0,)), ((), ())), preferred_element_type=F32)


def dot_nt(a, b):
    return lax.dot_general(a, b, (((1,), (1,)), ((), ())), preferred_element_type=F32)


def dot_tn(a, b):
    return lax.dot_general(a, b, (((0,), (0,)), ((), ())), preferred_element_type=F32)


def swap(a, axis, step=1):
    return lax.ppermute(a, axis, [(i, i ^ step) for i in range(lax.axis_size(axis))])


def shift(a, axis, step):
    n = lax.axis_size(axis)
    return lax.ppermute(a, axis, [(i, i + step) for i in range(n) if 0 <= i + step < n])


def pick(a, index, axis):
    return lax.dynamic_index_in_dim(a, index, axis, keepdims=False)


def after(value, *others):
    return lax.optimization_barrier((value,) + others)[0]


def gather_level(w):
    depth = lax.axis_size("z")
    return [w] + [swap(w, "z", j) for j in range(1, depth)]


def gather_rest(got):
    rows, cols = got[0].shape
    depth = len(got)
    z, y = lax.axis_index("z"), lax.axis_index("y")
    ordered = []
    for p in range(depth):
        v = got[0]
        for j in range(1, depth):
            v = jnp.where(z == (p ^ j), got[j], v)
        ordered.append(v)
    own = jnp.stack(ordered)
    other = swap(own, "y")
    block = jnp.stack([jnp.where(y == 0, own, other), jnp.where(y == 0, other, own)], axis=1)
    block = block.reshape(depth * 2 * rows, cols)
    near = jnp.stack([block, swap(block, "x")])
    return near, swap(near, "core")


def reduce_rows(acts, grads, dp):
    tokens, width = acts.shape
    cols = grads.shape[1]
    depth = lax.axis_size("z")
    z, y = lax.axis_index("z"), lax.axis_index("y")
    part = width // 4
    rows = part // (depth * 2)
    block = lambda d: lax.dynamic_slice_in_dim(acts, (dp ^ d) * part, part, 1)
    away = jnp.concatenate([block(1), block(3)], axis=1)
    got = swap(dot_tn(away, grads).astype(BF16), "core")
    far = (dot_tn(block(2), grads) + got[part:].astype(F32)).astype(BF16)
    far = swap(far, "x")
    near = dot_tn(block(0), grads) + got[:part].astype(F32)
    near = (near + far.astype(F32)).astype(BF16).reshape(depth, 2, rows, cols)
    far = swap(pick(near, 1 - y, 1), "y")
    near = (pick(near, y, 1).astype(F32) + far.astype(F32)).astype(BF16)
    total = pick(near, z, 0).astype(F32)
    for j in range(1, depth):
        total = total + swap(pick(near, z ^ j, 0), "z", j).astype(F32)
    return total


def project_kernel(place, x_ref, near_ref, far_ref, out_ref):
    part = near_ref.shape[1]
    total = None
    for d in range(4):
        cols = pl.ds(pl.multiple_of((place[0] ^ d) * part, part), part)
        weight = (far_ref if d & 1 else near_ref)[d >> 1]
        term = dot_nn(x_ref[:, cols], weight)
        total = term if total is None else total + term
    out_ref[...] = total.astype(out_ref.dtype)


def project(x, weight, place, kind):
    near, far = weight
    tokens, width = x.shape
    _, part, cols = near.shape
    tile = 512
    return pl.pallas_call(
        project_kernel,
        grid_spec=pltpu.PrefetchScalarGridSpec(
            num_scalar_prefetch=1,
            grid=(cols // tile,),
            in_specs=[
                pl.BlockSpec((tokens, width), lambda i, p: (0, 0)),
                pl.BlockSpec((2, part, tile), lambda i, p: (0, 0, i)),
                pl.BlockSpec((2, part, tile), lambda i, p: (0, 0, i)),
            ],
            out_specs=pl.BlockSpec((tokens, tile), lambda i, p: (0, i)),
        ),
        out_shape=jax.ShapeDtypeStruct((tokens, cols), kind),
        compiler_params=pltpu.CompilerParams(vmem_limit_bytes=50 << 20),
        cost_estimate=pl.CostEstimate(
            flops=2 * tokens * width * cols,
            transcendentals=0,
            bytes_accessed=2 * (tokens * width + width * cols + tokens * cols),
        ),
        name="project",
    )(place, x, near, far)


def project_back_kernel(place, *refs, count):
    grads, weights, out_ref = refs[:count], refs[count : 3 * count], refs[3 * count]

    def step(side):
        total = None
        for i in range(count):
            term = dot_nt(grads[i][...], weights[2 * i + side][0])
            total = term if total is None else total + term
        out_ref[...] = total.astype(out_ref.dtype)

    @pl.when(pl.program_id(0) < 2)
    def _():
        step(0)

    @pl.when(pl.program_id(0) >= 2)
    def _():
        step(1)


def project_back(grads, weights, place, kind):
    tokens, cols = grads[0].shape
    _, part, _ = weights[0][0].shape
    count = len(grads)
    return pl.pallas_call(
        functools.partial(project_back_kernel, count=count),
        grid_spec=pltpu.PrefetchScalarGridSpec(
            num_scalar_prefetch=1,
            grid=(4,),
            in_specs=[pl.BlockSpec((tokens, cols), lambda i, p: (0, 0))] * count
            + [
                pl.BlockSpec((1, part, cols), lambda i, p: (jnp.minimum(i, 1), 0, 0)),
                pl.BlockSpec((1, part, cols), lambda i, p: (jnp.maximum(i - 2, 0), 0, 0)),
            ]
            * count,
            out_specs=pl.BlockSpec((tokens, part), lambda i, p: (0, p[0] ^ ((i % 2) * 2 + i // 2))),
        ),
        out_shape=jax.ShapeDtypeStruct((tokens, 4 * part), kind),
        compiler_params=pltpu.CompilerParams(vmem_limit_bytes=58 << 20),
        cost_estimate=pl.CostEstimate(
            flops=8 * tokens * part * cols * count,
            transcendentals=0,
            bytes_accessed=2 * (tokens * cols + 4 * part * cols) * count + 8 * tokens * part,
        ),
        name="project_back",
    )(place, *grads, *[w for pair in weights for w in pair])


def feed_kernel(x_ref, cot_ref, pair_ref, down_ref, out_ref, grad_ref, act_ref, hid_ref):
    depth, units, part = pair_ref.shape
    units = units // 2
    cot = cot_ref[...]
    gate, up = None, None
    for level in range(depth):
        cols = x_ref[:, level * part : (level + 1) * part]
        first = dot_nt(pair_ref[level, :units, :], cols)
        second = dot_nt(pair_ref[level, units:, :], cols)
        gate = first if gate is None else gate + first
        up = second if up is None else up + second
    grad_act = dot_nt(down_ref[...], cot)
    sig = 1.0 / (1.0 + jnp.exp(-gate))
    silu = gate * sig
    act = (silu * up).astype(BF16)
    act_ref[...] = act
    grad_gate = (grad_act * up * (sig * (1.0 + gate * (1.0 - sig)))).astype(BF16)
    grad_up = (grad_act * silu).astype(BF16)
    hid_ref[:units, :] = grad_gate
    hid_ref[units:, :] = grad_up
    out_ref[...] = dot_tn(act, down_ref[...]).astype(BF16)
    for level in range(depth):
        both = dot_tn(grad_gate, pair_ref[level, :units, :])
        both = both + dot_tn(grad_up, pair_ref[level, units:, :])
        grad_ref[:, level * part : (level + 1) * part] = both.astype(BF16)


def feed(x, cot, pair, down):
    tokens, width = x.shape
    depth, units2, part = pair.shape
    units = units2 // 2
    tile = 256
    row = lambda n: pl.BlockSpec((tile, n), lambda i: (i, 0))
    col = lambda n: pl.BlockSpec((n, tile), lambda i: (0, i))
    return pl.pallas_call(
        feed_kernel,
        grid=(tokens // tile,),
        in_specs=[
            row(width),
            row(width),
            pl.BlockSpec(pair.shape, lambda i: (0, 0, 0)),
            pl.BlockSpec(down.shape, lambda i: (0, 0)),
        ],
        out_specs=[row(width), row(width), col(units), col(units2)],
        out_shape=[
            jax.ShapeDtypeStruct((tokens, width), BF16),
            jax.ShapeDtypeStruct((tokens, width), BF16),
            jax.ShapeDtypeStruct((units, tokens), BF16),
            jax.ShapeDtypeStruct((units2, tokens), BF16),
        ],
        compiler_params=pltpu.CompilerParams(vmem_limit_bytes=50 << 20),
        cost_estimate=pl.CostEstimate(
            flops=12 * tokens * width * units,
            transcendentals=tokens * units,
            bytes_accessed=2 * (4 * tokens * width + 3 * units * width + 3 * units * tokens),
        ),
        name="feed",
    )(x, cot, pair, down)


def feed_weights_kernel(x_ref, cot_ref, act_ref, hid_ref, pair_ref, down_ref):
    pair_ref[0] = dot_nn(hid_ref[...], x_ref[...]).astype(BF16)
    down = dot_nn(act_ref[...], cot_ref[...]).astype(BF16)
    hidden = down_ref.shape[1]
    for level in range(down_ref.shape[0]):
        down_ref[level] = down[level * hidden : (level + 1) * hidden]


def feed_weights(x, cot, act, hid, depth):
    tokens, width = x.shape
    units, units2 = act.shape[0], hid.shape[0]
    part = width // depth
    return pl.pallas_call(
        feed_weights_kernel,
        grid=(depth,),
        in_specs=[
            pl.BlockSpec((tokens, part), lambda i: (0, i)),
            pl.BlockSpec((tokens, part), lambda i: (0, i)),
            pl.BlockSpec(act.shape, lambda i: (0, 0)),
            pl.BlockSpec(hid.shape, lambda i: (0, 0)),
        ],
        out_specs=[
            pl.BlockSpec((1, units2, part), lambda i: (i, 0, 0)),
            pl.BlockSpec((depth, units // depth, part), lambda i: (0, 0, i)),
        ],
        out_shape=[
            jax.ShapeDtypeStruct((depth, units2, part), BF16),
            jax.ShapeDtypeStruct((depth, units // depth, width), BF16),
        ],
        compiler_params=pltpu.CompilerParams(vmem_limit_bytes=50 << 20),
        cost_estimate=pl.CostEstimate(
            flops=6 * tokens * width * units,
            transcendentals=0,
            bytes_accessed=2 * (2 * tokens * width + 3 * units * (tokens + width)),
        ),
        name="feed_weights",
    )(x, cot, act, hid)


def gather_group(a):
    half = a.shape[1] // 2
    first, second = a[:, :half], a[:, half:]
    first2 = jnp.stack([first, swap(first, "x")])
    second2 = jnp.stack([second, swap(second, "y")])
    first4 = jnp.stack([first2, swap(first2, "y")], axis=1)
    second4 = jnp.stack([second2, swap(second2, "x")])
    four = jnp.concatenate([first4, second4], axis=-1)
    return jnp.concatenate([four, swap(four, "core")]).reshape(-1, a.shape[1])


def reduce_group(partial, rows):
    width = partial.shape[1]
    half = width // 2
    parts = partial.reshape(2, 2, 2, rows, width)
    mine = parts[0].astype(F32) + swap(parts[1], "core").astype(F32)
    first, second = mine[..., :half], mine[..., half:]
    first = first[:, 0] + swap(first[:, 1].astype(BF16), "y").astype(F32)
    first = first[0] + swap(first[1].astype(BF16), "x").astype(F32)
    second = second[0] + swap(second[1].astype(BF16), "x").astype(F32)
    second = second[0] + swap(second[1].astype(BF16), "y").astype(F32)
    return jnp.concatenate([first, second], axis=-1)


LOG2E = 1.4426950408889634


def write_bias(query_ref, key_ref, bias_ref):
    query_code = query_ref[:, 0:1]
    query_pos = query_ref[:, 1:2]
    key_code = key_ref[0:1, :]
    key_pos = key_ref[1:2, :]
    key_valid = key_ref[2:3, :]
    allowed = (
        (query_code == key_code)
        & (key_pos <= query_pos)
        & ((key_valid == 1) | (key_pos == query_pos))
    )
    bias_ref[...] = jnp.where(allowed, 0.0, -1e30)


def forward_kernel(query_ref, key_ref, q_ref, k_ref, v_ref, out_ref, low_ref, bias_ref, *, scale):
    @pl.when(pl.program_id(0) == 0)
    def _():
        write_bias(query_ref, key_ref, bias_ref)

    scores = dot_nt(q_ref[...], k_ref[...])
    weights = jnp.exp2(scores * (scale * LOG2E) + bias_ref[...])
    totals = jnp.sum(weights, axis=-1, keepdims=True)
    unnorm = dot_nn(weights.astype(BF16), v_ref[...])
    attended = unnorm / totals
    out_ref[...] = attended
    low_ref[...] = attended.astype(BF16)


def backward_kernel(
    query_ref, key_ref, q_ref, k_ref, v_ref, att_ref, grad_ref, dq_ref, dk_ref, dv_ref, bias_ref, *, scale
):
    @pl.when(pl.program_id(0) == 0)
    def _():
        write_bias(query_ref, key_ref, bias_ref)

    q, k, v = q_ref[...], k_ref[...], v_ref[...]
    grad = grad_ref[...]
    scores = dot_nt(q, k)
    weights = jnp.exp2(scores * (scale * LOG2E) + bias_ref[...])
    totals = jnp.sum(weights, axis=-1, keepdims=True)
    grad_totals = -jnp.sum(grad * att_ref[...], axis=-1, keepdims=True) / totals
    grad_unnorm = (grad / totals).astype(BF16)
    grad_weights = dot_nt(grad_unnorm, v)
    grad_scores = (weights * (grad_weights + grad_totals)).astype(BF16)
    dq_ref[...] = (dot_nn(grad_scores, k) * scale).astype(BF16)
    dk_ref[...] = (dot_tn(grad_scores, q) * scale).astype(BF16)
    dv_ref[...] = dot_tn(weights.astype(BF16), grad_unnorm).astype(BF16)


def attention_specs(rows, keys):
    whole = lambda shape: pl.BlockSpec(shape, lambda h: (0, 0))
    head = lambda n: pl.BlockSpec((n, HEAD_DIM), lambda h: (0, h))
    return whole, head


def attend_forward(query_info, key_info, queries, keys, values):
    rows, width = queries.shape
    count = keys.shape[0]
    whole, head = attention_specs(rows, count)
    return pl.pallas_call(
        functools.partial(forward_kernel, scale=1.0 / math.sqrt(HEAD_DIM)),
        grid=(width // HEAD_DIM,),
        in_specs=[whole(query_info.shape), whole(key_info.shape), head(rows), head(count), head(count)],
        out_specs=[head(rows), head(rows)],
        out_shape=[
            jax.ShapeDtypeStruct((rows, width), F32),
            jax.ShapeDtypeStruct((rows, width), BF16),
        ],
        scratch_shapes=[pltpu.VMEM((rows, count), F32)],
        compiler_params=pltpu.CompilerParams(vmem_limit_bytes=40 << 20),
        cost_estimate=pl.CostEstimate(
            flops=4 * rows * count * width,
            transcendentals=rows * count * width // HEAD_DIM,
            bytes_accessed=2 * (2 * count + 4 * rows) * width,
        ),
        name="attend_forward",
    )(query_info, key_info, queries, keys, values)


def attend_backward(query_info, key_info, queries, keys, values, attended, grads):
    rows, width = queries.shape
    count = keys.shape[0]
    whole, head = attention_specs(rows, count)
    return pl.pallas_call(
        functools.partial(backward_kernel, scale=1.0 / math.sqrt(HEAD_DIM)),
        grid=(width // HEAD_DIM,),
        in_specs=[
            whole(query_info.shape),
            whole(key_info.shape),
            head(rows),
            head(count),
            head(count),
            head(rows),
            head(rows),
        ],
        out_specs=[head(rows), head(count), head(count)],
        out_shape=[
            jax.ShapeDtypeStruct((rows, width), BF16),
            jax.ShapeDtypeStruct((count, width), BF16),
            jax.ShapeDtypeStruct((count, width), BF16),
        ],
        scratch_shapes=[pltpu.VMEM((rows, count), F32)],
        compiler_params=pltpu.CompilerParams(vmem_limit_bytes=48 << 20),
        cost_estimate=pl.CostEstimate(
            flops=10 * rows * count * width,
            transcendentals=rows * count * width // HEAD_DIM,
            bytes_accessed=2 * (4 * count + 6 * rows) * width,
        ),
        name="attend_backward",
    )(query_info, key_info, queries, keys, values, attended, grads)


def shards(
    inputs,
    kv_input,
    segment_ids,
    valid_mask,
    w_query,
    w_key,
    w_value,
    w_out,
    w_gate,
    w_up,
    w_down,
    gain_attn,
    gain_ffn,
    cotangent,
):
    rows, width = inputs.shape
    x, core, z, y = (lax.axis_index(name) for name in ALL)
    depth = lax.axis_size("z")
    devices = 4 * depth * 2
    dp, fsdp = x * 2 + core, z * 2 + y
    group_rows = rows * depth * 2
    seq_length = min(SEQ_LEN, group_rows)
    wide = w_query.shape[0]
    hidden = w_down.shape[0]

    small = jnp.concatenate(
        [gain_attn.astype(F32), gain_ffn.astype(F32), segment_ids.astype(F32), valid_mask.astype(F32)]
    )
    small = lax.all_to_all(
        jnp.broadcast_to(small[None], (devices, small.shape[0])), ALL, 0, 0, tiled=True
    )
    full_gain_attn = small[:, :wide].reshape(-1)
    full_gain_ffn = small[:, wide : 2 * wide].reshape(-1)
    ids_all = lax.dynamic_slice_in_dim(small, dp * depth * 2, depth * 2, 0)[:, 2 * wide :]
    ids_all = ids_all.astype(jnp.int32)

    (kv_first, w_key_, w_down_) = lax.optimization_barrier((kv_input, w_key, w_down, small))[:3]
    place = jnp.reshape(dp, (1,)).astype(jnp.int32)

    reach = min(-(-(seq_length // 2 - 1) // (2 * rows)), depth - 1)
    levels = [kv_first]
    for _ in range(reach):
        levels.append(shift(levels[-1], "z", 1))
    others = [swap(level, "y") for level in levels]
    kv_halo = jnp.concatenate(levels + others)
    block_ids = []
    for other in range(2):
        for level in range(reach + 1):
            block_ids.append(2 * (z - level) + (y ^ other))
    key_pos, key_seg, key_valid = [], [], []
    for block in block_ids:
        here = pick(ids_all, jnp.maximum(block, 0), 0)
        key_seg.append(here[:rows])
        key_valid.append(here[rows:])
        key_pos.append(block * rows + jnp.arange(rows, dtype=jnp.int32))
    key_pos, key_seg, key_valid = (jnp.concatenate(v) for v in (key_pos, key_seg, key_valid))
    query_pos = fsdp * rows + jnp.arange(rows, dtype=jnp.int32)
    code = lambda seg, pos: seg * 4096 + pos // seq_length
    zeros = jnp.zeros_like(key_pos)
    key_info = jnp.stack([code(key_seg, key_pos), key_pos, key_valid] + [zeros] * 5)
    zeros = jnp.zeros_like(query_pos)
    query_info = jnp.stack([code(segment_ids, query_pos), query_pos] + [zeros] * 6, axis=1)

    level_key = gather_level(w_key_)
    level_value = gather_level(after(w_value, *level_key))
    level_query = gather_level(after(w_query, *level_value))
    level_out = gather_level(after(w_out, *level_query))
    full_key = gather_rest(level_key)
    full_value = gather_rest(level_value)
    full_query = gather_rest(level_query)
    full_out = gather_rest(level_out)

    def split_columns(w):
        return w.reshape(wide, 4, depth, 2, hidden).transpose(1, 3, 0, 2, 4)

    pair = jnp.stack([split_columns(w_gate), split_columns(w_up)], axis=2)
    pair = pair.reshape(8, 2 * wide, depth * hidden)
    pair = lax.all_to_all(pair, GROUP, 0, 0, tiled=True)
    pair = pair.reshape(8, 2, wide, depth * hidden).transpose(1, 3, 0, 2)
    pair = pair.reshape(2 * depth * hidden, 8 * wide)
    part_down = lax.all_gather(w_down_, "z", axis=0, tiled=False).reshape(depth * hidden, width)
    pair = lax.all_gather(pair, "z", axis=0, tiled=False)

    def by_level(a):
        return a.reshape(rows, 4, depth, 2 * wide).swapaxes(1, 2).reshape(rows, width)

    def by_dp(a):
        return a.reshape(rows, depth, 4, 2 * wide).swapaxes(1, 2).reshape(rows, width)

    cot_all = gather_group(after(cotangent, *level_out))

    stream = inputs.astype(F32)
    squares_in = jnp.sum(stream * stream, axis=-1, keepdims=True)
    factor_one = lax.rsqrt(squares_in / width + EPSILON)
    unit_one = stream * factor_one
    normed1 = (unit_one * full_gain_attn).astype(BF16)
    keys = project(kv_halo, full_key, place, BF16)
    values = project(kv_halo, full_value, place, BF16)
    queries = project(normed1, full_query, place, BF16)
    attended_f, attended = attend_forward(query_info, key_info, queries, keys, values)
    middle = stream + project(attended, full_out, place, F32)
    squares_mid = jnp.sum(middle * middle, axis=-1, keepdims=True)
    factor_two = lax.rsqrt(squares_mid / width + EPSILON)
    unit_two = middle * factor_two
    normed2 = by_level((unit_two * full_gain_ffn).astype(BF16))
    normed2 = gather_group(normed2)
    out_parts, grad_parts, act, hid = feed(normed2, cot_all, pair, part_down)
    grad_normed2 = by_dp(reduce_group(grad_parts, rows))

    grad_pair, grad_down = feed_weights(normed2, cot_all, act, hid, depth)
    share_down = lax.psum_scatter(grad_down, "z", scatter_dimension=0, tiled=True)
    share_down = share_down.reshape(hidden, width).astype(F32)
    grad_pair = lax.psum_scatter(grad_pair, "z", scatter_dimension=0, tiled=True)
    grad_pair = grad_pair.reshape(2 * depth * hidden, 8 * wide).T
    grad_pair = grad_pair.reshape(8, wide, 2 * depth * hidden)
    grad_pair = lax.all_to_all(grad_pair, GROUP, 0, 0, tiled=True)
    grad_pair = grad_pair.reshape(4, 2, wide, 2, depth, hidden).transpose(3, 2, 0, 4, 1, 5)
    grad_pair = grad_pair.reshape(2, wide, devices * hidden).astype(F32)
    share_gate, share_up = grad_pair[0], grad_pair[1]

    part_gain_ffn = jnp.sum(grad_normed2 * unit_two, axis=0)
    inner = grad_normed2 * full_gain_ffn
    grad_middle = cotangent.astype(F32) + factor_two * (
        inner - unit_two * jnp.mean(inner * unit_two, axis=-1, keepdims=True)
    )
    grad_branch = grad_middle.astype(BF16)
    result = middle + reduce_group(after(out_parts, grad_branch), rows)
    share_out = reduce_rows(attended, grad_branch, dp)
    grad_attended = project_back([grad_branch], [full_out], place, F32)
    grad_queries, grad_keys, grad_values = attend_backward(
        query_info, key_info, queries, keys, values, attended_f, grad_attended
    )
    grad_halo = project_back([grad_keys, grad_values], [full_key, full_value], place, BF16)
    grad_halo = grad_halo.reshape(2, reach + 1, rows, width)
    grad_levels = grad_halo[0].astype(F32) + swap(grad_halo[1], "y").astype(F32)
    back = grad_levels[reach]
    for level in reversed(range(reach)):
        back = grad_levels[level] + shift(back.astype(BF16), "z", -1).astype(F32)
    grad_kv_input = back
    share_key = reduce_rows(kv_halo, grad_keys, dp)
    share_value = reduce_rows(kv_halo, grad_values, dp)
    share_query = reduce_rows(normed1, grad_queries, dp)
    grad_normed1 = project_back([grad_queries], [full_query], place, F32)
    part_gain_attn = jnp.sum(grad_normed1 * unit_one, axis=0)
    inner = grad_normed1 * full_gain_attn
    grad_inputs = grad_middle + factor_one * (
        inner - unit_one * jnp.mean(inner * unit_one, axis=-1, keepdims=True)
    )

    valid = valid_mask.astype(F32)
    squares_out = jnp.sum(result * result, axis=-1)
    sums = jnp.stack(
        [
            jnp.sum(valid * squares_in[:, 0]),
            jnp.sum(valid * squares_mid[:, 0]),
            jnp.sum(valid * squares_out),
            jnp.sum(valid),
        ]
    )
    tiny = jnp.concatenate(
        [
            part_gain_attn.reshape(devices, wide),
            part_gain_ffn.reshape(devices, wide),
            jnp.broadcast_to(sums[None], (devices, 4)),
        ],
        axis=1,
    )
    tiny = jnp.sum(lax.all_to_all(tiny, ALL, 0, 0, tiled=True), axis=0)
    divisor = tiny[2 * wide + 3] * width
    rms_in = jnp.sqrt(tiny[2 * wide] / divisor)
    rms_mid = jnp.sqrt(tiny[2 * wide + 1] / divisor)
    rms_out = jnp.sqrt(tiny[2 * wide + 2] / divisor)
    return (
        result.astype(BF16),
        grad_inputs,
        grad_kv_input,
        share_query,
        share_key,
        share_value,
        share_out,
        share_gate,
        share_up,
        share_down,
        tiny[:wide],
        tiny[wide : 2 * wide],
        rms_in,
        rms_mid,
        rms_out,
    )


def solution(mesh):
    inner = Mesh(
        mesh.devices.reshape(2, mesh.shape["dp"] // 2, mesh.shape["fsdp"] // 2, 2), ALL
    )
    rows, flat = P(ALL, None), P(ALL)
    return jax.shard_map(
        shards,
        mesh=inner,
        in_specs=(rows, rows, flat, flat) + (rows,) * 7 + (flat, flat, rows),
        out_specs=(rows,) * 10 + (flat, flat, P(), P(), P()),
        check_vma=False,
    )
```

```python
import functools
import math

import jax
import jax.numpy as jnp
from jax import lax
from jax.experimental import pallas as pl
from jax.experimental.pallas import tpu as pltpu
from jax.sharding import Mesh
from jax.sharding import PartitionSpec as P

HEAD_DIM = 128
SEQ_LEN = 4096
EPSILON = 1e-06
ALL = ("x", "core", "z", "y")
GROUP = ("x", "core", "y")
F32 = jnp.float32
BF16 = jnp.bfloat16


def dot_nn(a, b):
    return lax.dot_general(a, b, (((1,), (0,)), ((), ())), preferred_element_type=F32)


def dot_nt(a, b):
    return lax.dot_general(a, b, (((1,), (1,)), ((), ())), preferred_element_type=F32)


def dot_tn(a, b):
    return lax.dot_general(a, b, (((0,), (0,)), ((), ())), preferred_element_type=F32)


def swap(a, axis, step=1):
    return lax.ppermute(a, axis, [(i, i ^ step) for i in range(lax.axis_size(axis))])


def shift(a, axis, step):
    n = lax.axis_size(axis)
    return lax.ppermute(a, axis, [(i, i + step) for i in range(n) if 0 <= i + step < n])


def pick(a, index, axis):
    return lax.dynamic_index_in_dim(a, index, axis, keepdims=False)


def after(value, *others):
    return lax.optimization_barrier((value,) + others)[0]


def together(*values):
    return lax.optimization_barrier(values)


def copy_kernel(x_ref, out_ref):
    out_ref[...] = x_ref[...]


def settle(x):
    rows, cols = x.shape
    tile = 512 if cols % 512 == 0 else cols
    spec = pl.BlockSpec((rows, tile), lambda i: (0, i))
    return pl.pallas_call(
        copy_kernel,
        grid=(cols // tile,),
        in_specs=[spec],
        out_specs=spec,
        out_shape=jax.ShapeDtypeStruct(x.shape, x.dtype),
        name="settle",
    )(x)


def take_block(a, d, dp):
    part = a.shape[1] // 4
    return lax.dynamic_slice_in_dim(a, (dp ^ d) * part, part, 1)


def columns(acts, first, second, dp):
    return jnp.concatenate([take_block(acts, first, dp), take_block(acts, second, dp)], axis=1).T


def weight_grad_kernel(*refs, parts):
    outs = refs[len(refs) - parts :]
    total = dot_nn(refs[0][...], refs[1][...])
    if len(refs) - parts == 3:
        total = total + refs[2][...].astype(F32)
    rows = outs[0].shape[0]
    for i, out in enumerate(outs):
        out[...] = total[i * rows : (i + 1) * rows].astype(BF16)


def weight_grad(acts, grads, got=None, parts=1):
    rows, tokens = acts.shape
    cols = grads.shape[1]
    tile = 512
    col = lambda n: pl.BlockSpec((n, tile), lambda i: (0, i))
    args = (acts, grads) if got is None else (acts, grads, got)
    out = pl.pallas_call(
        functools.partial(weight_grad_kernel, parts=parts),
        grid=(cols // tile,),
        in_specs=[pl.BlockSpec(acts.shape, lambda i: (0, 0)), col(tokens), col(rows)][: len(args)],
        out_specs=[col(rows // parts)] * parts,
        out_shape=[jax.ShapeDtypeStruct((rows // parts, cols), BF16)] * parts,
        compiler_params=pltpu.CompilerParams(vmem_limit_bytes=40 << 20),
        cost_estimate=pl.CostEstimate(
            flops=2 * rows * tokens * cols,
            transcendentals=0,
            bytes_accessed=2 * (rows * tokens + tokens * cols + 2 * rows * cols),
        ),
        name="weight_grad",
    )(*args)
    return out if parts > 1 else out[0]


def by_owner(near):
    depth = lax.axis_size("z")
    return near.reshape(depth, 2, -1, near.shape[1])


def add(a, b):
    return (a.astype(F32) + b.astype(F32)).astype(BF16)


def split_y(a):
    y = lax.axis_index("y")
    return pick(a, 1 - y, a.ndim - 3), pick(a, y, a.ndim - 3)


def collect(a):
    out = lax.psum_scatter(a, "z", scatter_dimension=0, tiled=True)
    return out.reshape(out.shape[1:]).astype(F32)


def project_kernel(*refs):
    weight_ref, out_ref = refs[-2:]
    at = 0
    for x_ref in refs[:-2]:
        rows = x_ref.shape[0]
        out_ref[at : at + rows, :] = dot_nn(x_ref[...], weight_ref[...]).astype(out_ref.dtype)
        at += rows


def project(pieces, weights, first, count, kind):
    rows, width = pieces[0].shape
    tokens, cols = rows * len(pieces), count * width
    tile = 512
    return pl.pallas_call(
        project_kernel,
        grid=(cols // tile,),
        in_specs=[pl.BlockSpec((rows, width), lambda i: (0, 0))] * len(pieces)
        + [pl.BlockSpec((width, tile), lambda i: (0, first * (width // tile) + i))],
        out_specs=pl.BlockSpec((tokens, tile), lambda i: (0, i)),
        out_shape=jax.ShapeDtypeStruct((tokens, cols), kind),
        compiler_params=pltpu.CompilerParams(vmem_limit_bytes=50 << 20),
        cost_estimate=pl.CostEstimate(
            flops=2 * tokens * width * cols,
            transcendentals=0,
            bytes_accessed=2 * (tokens * width + width * cols + tokens * cols),
        ),
        name="project",
    )(*pieces, weights)


def project_back_kernel(*refs, count):
    total = None
    for i in range(count):
        term = dot_nt(refs[i][...], refs[count + i][...])
        total = term if total is None else total + term
    refs[-1][...] = total.astype(refs[-1].dtype)


def project_back(grads, weights, numbers, kind):
    tokens, width = grads[0].shape
    tile = 512
    count = len(grads)
    weight = lambda number: pl.BlockSpec((tile, width), lambda i: (i, number))
    return pl.pallas_call(
        functools.partial(project_back_kernel, count=count),
        grid=(width // tile,),
        in_specs=[pl.BlockSpec((tokens, width), lambda i: (0, 0))] * count
        + [weight(number) for number in numbers],
        out_specs=pl.BlockSpec((tokens, tile), lambda i: (0, i)),
        out_shape=jax.ShapeDtypeStruct((tokens, width), kind),
        compiler_params=pltpu.CompilerParams(vmem_limit_bytes=58 << 20),
        cost_estimate=pl.CostEstimate(
            flops=2 * tokens * width * width * count,
            transcendentals=0,
            bytes_accessed=2 * (tokens + width) * width * count + 4 * tokens * width,
        ),
        name="project_back",
    )(*grads, *[weights] * count)


def level_spans(width, depth, natural):
    part = width // depth
    if not natural:
        return [[(level * part, part)] for level in range(depth)]
    piece = part // 4
    return [[((p * depth + level) * piece, piece) for p in range(4)] for level in range(depth)]


def feed_kernel(x_ref, cot_ref, pair_ref, down_ref, *refs, spans, summed):
    units = down_ref.shape[0]
    gate, up = None, None
    for level, pieces in enumerate(spans):
        cols = [x_ref[:, start : start + size] for start, size in pieces]
        cols = cols[0] if len(cols) == 1 else jnp.concatenate(cols, axis=1)
        first = dot_nt(pair_ref[level, :units, :], cols)
        second = dot_nt(pair_ref[level, units : 2 * units, :], cols)
        gate = first if gate is None else gate + first
        up = second if up is None else up + second
    grad_act = dot_nt(down_ref[...], cot_ref[...])
    sig = 1.0 / (1.0 + jnp.exp(-gate))
    silu = gate * sig
    act = (silu * up).astype(BF16)
    grad_gate = (grad_act * up * (sig * (1.0 + gate * (1.0 - sig)))).astype(BF16)
    grad_up = (grad_act * silu).astype(BF16)
    act_ref, hid_ref = refs[-2:] if not summed else refs[2:4]
    act_ref[...] = act
    hid_ref[:units, :] = grad_gate
    hid_ref[units:, :] = grad_up
    if summed:
        grad_got, grad_ref = refs[0], refs[8]
    else:
        grad_ref = refs[1]
    out_ref = refs[1 if summed else 0]
    out_ref[...] = dot_tn(act, down_ref[...]).astype(BF16)
    for level, pieces in enumerate(spans):
        both = dot_tn(grad_gate, pair_ref[level, :units, :])
        both = both + dot_tn(grad_up, pair_ref[level, units : 2 * units, :])
        at = 0
        for start, size in pieces:
            term = both[:, at : at + size]
            if summed:
                term = term + grad_got[:, start : start + size].astype(F32)
            grad_ref[:, start : start + size] = term.astype(grad_ref.dtype)
            at += size
    if summed:
        step = pl.program_id(0)
        half = grad_ref.shape[1] // 2
        for number, (mine, cols) in enumerate(
            (
                (step % 2 == 0, slice(0, half)),
                (step % 2 == 1, slice(0, half)),
                (step < 2, slice(half, 2 * half)),
                (step >= 2, slice(half, 2 * half)),
            )
        ):

            @pl.when(mine)
            def _(piece=refs[4 + number], cols=cols):
                piece[0] = grad_ref[:, cols].astype(BF16)


def feed(x, cot, pair, down, natural, got=None):
    tokens, width = x.shape
    depth, units = pair.shape[0], down.shape[0]
    units2 = 2 * units
    tile = tokens // 4
    half = width // 2
    summed = got is not None
    row = lambda n: pl.BlockSpec((tile, n), lambda i: (i, 0))
    col = lambda n: pl.BlockSpec((n, tile), lambda i: (0, i))
    piece = lambda at: pl.BlockSpec((1, tile, half), lambda i: (at(i), 0, 0))
    pieces = [
        piece(lambda i: i // 2),
        piece(lambda i: i // 2),
        piece(lambda i: jnp.minimum(i, 1)),
        piece(lambda i: jnp.maximum(i - 2, 0)),
    ]
    big = [jax.ShapeDtypeStruct((tokens, width), BF16)] * 2
    sums = [jax.ShapeDtypeStruct((2, tile, half), BF16)] * 4
    acts = [
        jax.ShapeDtypeStruct((units, tokens), BF16),
        jax.ShapeDtypeStruct((units2, tokens), BF16),
    ]
    acts_specs = [col(units), col(units2)]
    return pl.pallas_call(
        functools.partial(
            feed_kernel, spans=level_spans(width, depth, natural), summed=summed
        ),
        grid=(4,),
        in_specs=[
            row(width),
            row(width),
            pl.BlockSpec(pair.shape, lambda i: (0, 0, 0)),
            pl.BlockSpec(down.shape, lambda i: (0, 0)),
        ]
        + ([row(width)] if summed else []),
        out_specs=[row(width)] + (acts_specs + pieces if summed else [row(width)] + acts_specs),
        out_shape=big[:1] + acts + sums if summed else big + acts,
        scratch_shapes=[pltpu.VMEM((tile, width), F32)] if summed else [],
        compiler_params=pltpu.CompilerParams(vmem_limit_bytes=56 << 20),
        cost_estimate=pl.CostEstimate(
            flops=12 * tokens * width * units,
            transcendentals=tokens * units,
            bytes_accessed=2 * (4 * tokens * width + 3 * units * width + 3 * units * tokens),
        ),
        name="feed_sum" if summed else "feed",
    )(x, cot, pair, down, *((got,) if summed else ()))


def feed_weights_kernel(*refs, count):
    pair_ref, down_ref = refs[4 * count :]
    pair, down = None, None
    for i in range(count):
        x_ref, cot_ref, act_ref, hid_ref = refs[4 * i : 4 * i + 4]
        first = dot_nn(hid_ref[...], x_ref[...])
        second = dot_nn(act_ref[...], cot_ref[...])
        pair = first if pair is None else pair + first
        down = second if down is None else down + second
    pair, down = pair.astype(BF16), down.astype(BF16)
    for level in range(pair_ref.shape[0]):
        size = pair_ref.shape[2]
        pair_ref[level] = pair[:, level * size : (level + 1) * size]
    for level in range(down_ref.shape[0]):
        size = down_ref.shape[1]
        down_ref[level] = down[level * size : (level + 1) * size]


def feed_weights(sets, depth, natural):
    x, _, act, hid = sets[0]
    tokens, width = x.shape
    units, units2 = act.shape[0], hid.shape[0]
    steps = 4 if natural else depth
    part = width // steps
    if natural:
        pair_spec = pl.BlockSpec((depth, units2, part // depth), lambda i: (0, 0, i))
    else:
        pair_spec = pl.BlockSpec((1, units2, part), lambda i: (i, 0, 0))
    return pl.pallas_call(
        functools.partial(feed_weights_kernel, count=len(sets)),
        grid=(steps,),
        in_specs=[
            pl.BlockSpec((tokens, part), lambda i: (0, i)),
            pl.BlockSpec((tokens, part), lambda i: (0, i)),
            pl.BlockSpec(act.shape, lambda i: (0, 0)),
            pl.BlockSpec(hid.shape, lambda i: (0, 0)),
        ]
        * len(sets),
        out_specs=[
            pair_spec,
            pl.BlockSpec((depth, units // depth, part), lambda i: (0, 0, i)),
        ],
        out_shape=[
            pltpu.HBM((depth, units2, width // depth), BF16),
            pltpu.HBM((depth, units // depth, width), BF16),
        ],
        compiler_params=pltpu.CompilerParams(vmem_limit_bytes=50 << 20),
        cost_estimate=pl.CostEstimate(
            flops=6 * tokens * width * units * len(sets),
            transcendentals=0,
            bytes_accessed=2 * (2 * tokens * width + 3 * units * tokens) * len(sets)
            + 6 * units * width,
        ),
        name="feed_weights",
    )(*[v for group in sets for v in group])


def reduce_last(first, first_y, second, second_x):
    first, second = add(first, first_y), add(second, second_x)
    return first[0], first[1], second[0], second[1]


def reduce_done(first, first_x, second, second_y):
    first = first.astype(F32) + first_x.astype(F32)
    second = second.astype(F32) + second_y.astype(F32)
    return jnp.concatenate([first, second], axis=-1)


LOG2E = 1.4426950408889634


def write_bias(query_ref, key_ref, bias_ref):
    query_code = query_ref[:, 0:1]
    query_pos = query_ref[:, 1:2]
    key_code = key_ref[0:1, :]
    key_pos = key_ref[1:2, :]
    key_valid = key_ref[2:3, :]
    allowed = (
        (query_code == key_code)
        & (key_pos <= query_pos)
        & ((key_valid == 1) | (key_pos == query_pos))
    )
    bias_ref[...] = jnp.where(allowed, 0.0, -1e30)


def forward_kernel(query_ref, key_ref, q_ref, k_ref, v_ref, out_ref, low_ref, bias_ref, *, scale):
    @pl.when(pl.program_id(0) == 0)
    def _():
        write_bias(query_ref, key_ref, bias_ref)

    scores = dot_nt(q_ref[...], k_ref[...])
    weights = jnp.exp2(scores * (scale * LOG2E) + bias_ref[...])
    totals = jnp.sum(weights, axis=-1, keepdims=True)
    unnorm = dot_nn(weights.astype(BF16), v_ref[...])
    attended = unnorm / totals
    out_ref[...] = attended
    low_ref[...] = attended.astype(BF16)


def backward_kernel(
    query_ref, key_ref, q_ref, k_ref, v_ref, att_ref, grad_ref, dq_ref, dk_ref, dv_ref, bias_ref, *, scale
):
    @pl.when(pl.program_id(0) == 0)
    def _():
        write_bias(query_ref, key_ref, bias_ref)

    q, k, v = q_ref[...], k_ref[...], v_ref[...]
    grad = grad_ref[...]
    scores = dot_nt(q, k)
    weights = jnp.exp2(scores * (scale * LOG2E) + bias_ref[...])
    totals = jnp.sum(weights, axis=-1, keepdims=True)
    grad_totals = -jnp.sum(grad * att_ref[...], axis=-1, keepdims=True) / totals
    grad_unnorm = (grad / totals).astype(BF16)
    grad_weights = dot_nt(grad_unnorm, v)
    grad_scores = (weights * (grad_weights + grad_totals)).astype(BF16)
    dq_ref[...] = (dot_nn(grad_scores, k) * scale).astype(BF16)
    dk_ref[...] = (dot_tn(grad_scores, q) * scale).astype(BF16)
    dv_ref[...] = dot_tn(weights.astype(BF16), grad_unnorm).astype(BF16)


def attention_specs(rows, keys):
    whole = lambda shape: pl.BlockSpec(shape, lambda h: (0, 0))
    head = lambda n, first=0: pl.BlockSpec((n, HEAD_DIM), lambda h: (0, first + h))
    return whole, head


def attend_forward(query_info, key_info, queries, pairs):
    rows, width = queries.shape
    count = pairs.shape[0]
    whole, head = attention_specs(rows, count)
    return pl.pallas_call(
        functools.partial(forward_kernel, scale=1.0 / math.sqrt(HEAD_DIM)),
        grid=(width // HEAD_DIM,),
        in_specs=[
            whole(query_info.shape),
            whole(key_info.shape),
            head(rows),
            head(count),
            head(count, width // HEAD_DIM),
        ],
        out_specs=[head(rows), head(rows)],
        out_shape=[
            jax.ShapeDtypeStruct((rows, width), F32),
            jax.ShapeDtypeStruct((rows, width), BF16),
        ],
        scratch_shapes=[pltpu.VMEM((rows, count), F32)],
        compiler_params=pltpu.CompilerParams(vmem_limit_bytes=40 << 20),
        cost_estimate=pl.CostEstimate(
            flops=4 * rows * count * width,
            transcendentals=rows * count * width // HEAD_DIM,
            bytes_accessed=2 * (2 * count + 4 * rows) * width,
        ),
        name="attend_forward",
    )(query_info, key_info, queries, pairs, pairs)


def attend_backward(query_info, key_info, queries, pairs, attended, grads):
    rows, width = queries.shape
    count = pairs.shape[0]
    whole, head = attention_specs(rows, count)
    return pl.pallas_call(
        functools.partial(backward_kernel, scale=1.0 / math.sqrt(HEAD_DIM)),
        grid=(width // HEAD_DIM,),
        in_specs=[
            whole(query_info.shape),
            whole(key_info.shape),
            head(rows),
            head(count),
            head(count, width // HEAD_DIM),
            head(rows),
            head(rows),
        ],
        out_specs=[head(rows), head(count), head(count)],
        out_shape=[
            jax.ShapeDtypeStruct((rows, width), BF16),
            jax.ShapeDtypeStruct((count, width), BF16),
            jax.ShapeDtypeStruct((count, width), BF16),
        ],
        scratch_shapes=[pltpu.VMEM((rows, count), F32)],
        compiler_params=pltpu.CompilerParams(vmem_limit_bytes=48 << 20),
        cost_estimate=pl.CostEstimate(
            flops=10 * rows * count * width,
            transcendentals=rows * count * width // HEAD_DIM,
            bytes_accessed=2 * (4 * count + 6 * rows) * width,
        ),
        name="attend_backward",
    )(query_info, key_info, queries, pairs, pairs, attended, grads)


def shards(
    inputs,
    kv_input,
    segment_ids,
    valid_mask,
    w_query,
    w_key,
    w_value,
    w_out,
    w_gate,
    w_up,
    w_down,
    gain_attn,
    gain_ffn,
    cotangent,
):
    rows, width = inputs.shape
    x, core, z, y = (lax.axis_index(name) for name in ALL)
    depth = lax.axis_size("z")
    devices = 4 * depth * 2
    dp, fsdp = x * 2 + core, z * 2 + y
    group_rows = rows * depth * 2
    seq_length = min(SEQ_LEN, group_rows)
    wide = w_query.shape[0]
    hidden = w_down.shape[0]

    small = jnp.concatenate(
        [gain_attn.astype(F32), gain_ffn.astype(F32), segment_ids.astype(F32), valid_mask.astype(F32)]
    )
    small = lax.all_to_all(
        jnp.broadcast_to(small[None], (devices, small.shape[0])), ALL, 0, 0, tiled=True
    )
    reach = min(-(-(seq_length // 2 - 1) // (2 * rows)), depth - 1)
    natural = 2 * wide % 128 == 0


    weights = jnp.concatenate([w_key, w_value, w_query, w_out], axis=1)
    weights = lax.all_gather(weights, ALL, axis=0, tiled=True)
    levels = [kv_input, shift(kv_input, "z", 1)]
    others = [swap(kv_input, "y")]

    def split_columns(w):
        return w.reshape(wide, 4, depth, 2, hidden).transpose(1, 3, 0, 2, 4)

    pair = jnp.stack([split_columns(w_gate), split_columns(w_up)], axis=2)
    pair = pair.reshape(8, 2 * wide, depth * hidden)
    levels[1], others[0], pair = together(levels[1], others[0], pair)

    others.append(swap(levels[1], "y"))
    for _ in range(reach - 1):
        levels.append(shift(levels[-1], "z", 1))
    for level in levels[2:-1]:
        others.append(swap(level, "y"))
    pair = lax.all_to_all(pair, GROUP, 0, 0, tiled=True)
    pair, *held = together(pair, *others, *levels[1:])
    others, levels = held[: len(others)], [kv_input] + held[len(others) :]

    if len(others) < len(levels):
        others.append(swap(levels[-1], "y"))
    pair = pair.reshape(8, 2, wide, depth * hidden).transpose(1, 3, 0, 2)
    pair = settle(pair.reshape(2 * depth * hidden, 8 * wide))
    pair, small, weights, cot_first, down, *halo = together(
        pair, small, weights, cotangent, w_down, *levels, *others
    )

    pair = lax.all_gather(pair, "z", axis=0, tiled=False)
    cot_y = swap(cot_first, "y")
    pairs = project(halo, weights, 0, 2, BF16)
    cot_y, pairs = together(cot_y, pairs)
    cot_pair = jnp.concatenate([cot_first, cot_y])
    cot_x = swap(cot_pair, "x")
    full_gain_attn = small[:, :wide].reshape(-1)
    full_gain_ffn = small[:, wide : 2 * wide].reshape(-1)
    ids_all = lax.dynamic_slice_in_dim(small, dp * depth * 2, depth * 2, 0)[:, 2 * wide :]
    ids_all = ids_all.astype(jnp.int32)
    block_ids = []
    for other in range(2):
        for level in range(reach + 1):
            block_ids.append(2 * (z - level) + (y ^ other))
    key_pos, key_seg, key_valid = [], [], []
    for block in block_ids:
        here = pick(ids_all, jnp.maximum(block, 0), 0)
        key_seg.append(here[:rows])
        key_valid.append(here[rows:])
        key_pos.append(block * rows + jnp.arange(rows, dtype=jnp.int32))
    key_pos, key_seg, key_valid = (jnp.concatenate(v) for v in (key_pos, key_seg, key_valid))
    query_pos = fsdp * rows + jnp.arange(rows, dtype=jnp.int32)
    code = lambda seg, pos: seg * 4096 + pos // seq_length
    zeros = jnp.zeros_like(key_pos)
    key_info = jnp.stack([code(key_seg, key_pos), key_pos, key_valid] + [zeros] * 5)
    zeros = jnp.zeros_like(query_pos)
    query_info = jnp.stack([code(segment_ids, query_pos), query_pos] + [zeros] * 6, axis=1)
    stream = inputs.astype(F32)
    squares_in = jnp.sum(stream * stream, axis=-1, keepdims=True)
    factor_one = lax.rsqrt(squares_in / width + EPSILON)
    unit_one = stream * factor_one
    normed1 = (unit_one * full_gain_attn).astype(BF16)
    queries = project([normed1], weights, 2, 1, BF16)
    attended_f, attended = attend_forward(query_info, key_info, queries, pairs)
    middle = stream + project([attended], weights, 3, 1, F32)
    squares_mid = jnp.sum(middle * middle, axis=-1, keepdims=True)
    factor_two = lax.rsqrt(squares_mid / width + EPSILON)
    unit_two = middle * factor_two
    normed2 = (unit_two * full_gain_ffn).astype(BF16)
    if not natural:
        normed2 = normed2.reshape(rows, 4, depth, 2 * wide).swapaxes(1, 2).reshape(rows, width)
    half = width // 2
    first, second, cot_x, pair, down = together(
        normed2[:, :half], normed2[:, half:], cot_x, pair, down
    )
    part_down = lax.all_gather(down, "z", axis=0, tiled=False)
    cot_near = jnp.concatenate([cot_pair, cot_x])
    cot_far = swap(cot_near, "core")

    halo = jnp.concatenate(halo)
    first_x, second_y = swap(first, "x"), swap(second, "y")
    halo_far, halo_near = columns(halo, 1, 3, dp), columns(halo, 0, 2, dp)
    first_x, second_y, halo_far, halo_near, cot_near, cot_far = together(
        first_x, second_y, halo_far, halo_near, cot_near, cot_far
    )
    first, second = jnp.stack([first, first_x]), jnp.stack([second, second_y])
    first_y, second_x = swap(first, "y"), swap(second, "x")
    part_down = part_down.reshape(depth * hidden, width)
    attended_far, attended_near = columns(attended, 1, 3, dp), columns(attended, 0, 2, dp)
    normed1_far, normed1_near = columns(normed1, 1, 3, dp), columns(normed1, 0, 2, dp)
    (
        first_y, second_x, part_down, attended_far, attended_near, normed1_far, normed1_near,
    ) = together(
        first_y, second_x, part_down, attended_far, attended_near, normed1_far, normed1_near,
    )
    first = jnp.stack([first, first_y], axis=1)
    second = jnp.stack([second, second_x])
    x_near = jnp.concatenate([first, second], axis=-1).reshape(4 * rows, width)
    x_far = swap(x_near, "core")
    feeds = pair

    out_far, grad_far, act_far, hid_far = feed(x_far, cot_far, feeds, part_down, natural)
    got = swap(grad_far, "core")
    out_near, act_near, hid_near, first, first_away, second, second_away = feed(
        x_near, cot_near, feeds, part_down, natural, got
    )
    out_got = swap(out_far, "core")
    first_y, second_x = swap(first_away, "y"), swap(second_away, "x")
    grad_pair, grad_down = feed_weights(
        [(x_near, cot_near, act_near, hid_near), (x_far, cot_far, act_far, hid_far)], depth, natural
    )
    first, first_away, second, second_away = reduce_last(first, first_y, second, second_x)
    first, first_away, second, second_away, grad_pair, grad_down, out_near, out_got = together(
        first, first_away, second, second_away, grad_pair, grad_down, out_near, out_got
    )
    grad_pair = lax.psum_scatter(grad_pair, "z", scatter_dimension=0, tiled=True)
    share_down = collect(grad_down)
    first_x, second_y = swap(first_away, "x"), swap(second_away, "y")
    grad_normed2 = reduce_done(first, first_x, second, second_y)
    if not natural:
        grad_normed2 = grad_normed2.reshape(rows, depth, 4, 2 * wide).swapaxes(1, 2)
        grad_normed2 = grad_normed2.reshape(rows, width)

    part_gain_ffn = jnp.sum(grad_normed2 * unit_two, axis=0)
    inner = grad_normed2 * full_gain_ffn
    grad_middle = cotangent.astype(F32) + factor_two * (
        inner - unit_two * jnp.mean(inner * unit_two, axis=-1, keepdims=True)
    )
    grad_branch = grad_middle.astype(BF16)
    far_out = weight_grad(attended_far, grad_branch)
    far_out, grad_branch, grad_middle = together(far_out, grad_branch, grad_middle)
    got_out = swap(far_out, "core")
    grad_attended = project_back([grad_branch], weights, [3], F32)
    out_home, out_away = weight_grad(attended_near, grad_branch, got_out, 2)
    out_home, out_away, grad_attended = together(out_home, out_away, grad_attended)

    out_x = swap(out_away, "x")
    grad_queries, grad_keys, grad_values = attend_backward(
        query_info, key_info, queries, pairs, attended_f, grad_attended
    )
    far_key = weight_grad(halo_far, grad_keys)
    out_x, far_key, grad_keys, grad_values, grad_queries = together(
        out_x, far_key, grad_keys, grad_values, grad_queries
    )

    got_key = swap(far_key, "core")
    far_value = weight_grad(halo_far, grad_values)
    got_key, far_value, grad_keys, grad_values, grad_queries = together(
        got_key, far_value, grad_keys, grad_values, grad_queries
    )

    got_value = swap(far_value, "core")
    key_home, key_away = weight_grad(halo_near, grad_keys, got_key, 2)
    got_value, key_home, key_away, grad_keys, grad_values, grad_queries, grad_pair = together(
        got_value, key_home, key_away, grad_keys, grad_values, grad_queries, grad_pair
    )

    key_x = swap(key_away, "x")
    out_away, out_home = split_y(by_owner(add(out_home, out_x)))
    out_y = swap(out_away, "y")
    value_near = weight_grad(halo_near, grad_values, got_value)
    far_query = weight_grad(normed1_far, grad_queries)
    grad_halo = project_back([grad_keys, grad_values], weights, [0, 1], BF16)
    query_home, query_away = weight_grad(normed1_near, grad_queries, swap(far_query, "core"), 2)
    grad_pair = settle(grad_pair.reshape(2 * depth * hidden, 8 * wide)).T
    key_x, out_y, value_near, query_home, query_away, grad_halo, grad_queries, grad_pair = together(
        key_x, out_y, value_near, query_home, query_away, grad_halo, grad_queries, grad_pair
    )

    value_away, value_home = split_y(value_near.reshape(2, depth, 2, wide, width))
    query_x, value_y = swap(query_away, "x"), swap(value_away, "y")
    grad_halo = grad_halo.reshape(2, reach + 1, rows, width)
    back = grad_halo[:, reach]
    for level in reversed(range(1, reach)):
        back = shift(back, "z", -1)
        back = add(grad_halo[:, level], back) if level > 1 else back
    share_out = collect(add(out_home, out_y))
    grad_normed1 = project_back([grad_queries], weights, [2], F32)
    grad_pair = settle(grad_pair).reshape(8, wide, 2 * depth * hidden)
    grad_pair = lax.all_to_all(grad_pair, GROUP, 0, 0, tiled=True)
    query_x, value_y, back, grad_normed1, grad_pair = together(
        query_x, value_y, back, grad_normed1, grad_pair
    )

    key_away, key_home = split_y(by_owner(add(key_home, key_x)))
    query_away, query_home = split_y(by_owner(add(query_home, query_x)))
    value_home = add(value_home, value_y)
    key_y, query_y, value_x = swap(key_away, "y"), swap(query_away, "y"), swap(value_home[1], "x")
    if reach > 1:
        back = add(grad_halo[:, 1], back)
    back = shift(back, "z", -1)
    part_gain_attn = jnp.sum(grad_normed1 * unit_one, axis=0)
    inner = grad_normed1 * full_gain_attn
    grad_inputs = grad_middle + factor_one * (
        inner - unit_one * jnp.mean(inner * unit_one, axis=-1, keepdims=True)
    )
    grad_pair = grad_pair.reshape(4, 2, wide, 2, depth, hidden).transpose(3, 2, 0, 4, 1, 5)
    grad_pair = grad_pair.reshape(2, wide, devices * hidden).astype(F32)
    sums = add(out_near, out_got).reshape(2, 2, rows, width)
    sums = sums[:, 0, :, :half], sums[:, 1, :, :half], sums[0, :, :, half:], sums[1, :, :, half:]
    key_y, query_y, value_x, back, grad_inputs, share_gate, share_up, *sums = together(
        key_y, query_y, value_x, back, grad_inputs, grad_pair[0], grad_pair[1], *sums
    )

    shares = jnp.concatenate(
        [add(key_home, key_y), add(value_home[0], value_x), add(query_home, query_y)], axis=1
    )
    shares = lax.psum_scatter(shares, "z", scatter_dimension=0, tiled=True)[0].astype(F32)
    sum_y, sum_x = swap(sums[1], "y"), swap(sums[3], "x")
    back = add(grad_halo[:, 0], back)
    sum_y, sum_x, back = together(sum_y, sum_x, back)
    sums = reduce_last(sums[0], sum_y, sums[2], sum_x)
    back_y = swap(back[1], "y")
    sum_x, sum_y = together(swap(sums[1], "x"), swap(sums[3], "y"))
    grad_kv_input = back[0].astype(F32) + back_y.astype(F32)
    result = middle + reduce_done(sums[0], sum_x, sums[2], sum_y)
    valid = valid_mask.astype(F32)
    squares_out = jnp.sum(result * result, axis=-1)
    sums = jnp.stack(
        [
            jnp.sum(valid * squares_in[:, 0]),
            jnp.sum(valid * squares_mid[:, 0]),
            jnp.sum(valid * squares_out),
            jnp.sum(valid),
        ]
    )
    tiny = jnp.concatenate(
        [
            part_gain_attn.reshape(devices, wide),
            part_gain_ffn.reshape(devices, wide),
            jnp.broadcast_to(sums[None], (devices, 4)),
        ],
        axis=1,
    )
    tiny = lax.all_to_all(tiny, ALL, 0, 0, tiled=True)
    share_key, share_value, share_query = (
        shares[i * wide : (i + 1) * wide] for i in range(3)
    )

    tiny = jnp.sum(tiny, axis=0)
    divisor = tiny[2 * wide + 3] * width
    rms_in = jnp.sqrt(tiny[2 * wide] / divisor)
    rms_mid = jnp.sqrt(tiny[2 * wide + 1] / divisor)
    rms_out = jnp.sqrt(tiny[2 * wide + 2] / divisor)
    return (
        result.astype(BF16),
        grad_inputs,
        grad_kv_input,
        share_query,
        share_key,
        share_value,
        share_out,
        share_gate,
        share_up,
        share_down,
        tiny[:wide],
        tiny[wide : 2 * wide],
        rms_in,
        rms_mid,
        rms_out,
    )


def solution(mesh):
    inner = Mesh(
        mesh.devices.reshape(2, mesh.shape["dp"] // 2, mesh.shape["fsdp"] // 2, 2), ALL
    )
    rows, flat = P(ALL, None), P(ALL)
    return jax.shard_map(
        shards,
        mesh=inner,
        in_specs=(rows, rows, flat, flat) + (rows,) * 7 + (flat, flat, rows),
        out_specs=(rows,) * 10 + (flat, flat, P(), P(), P()),
        check_vma=False,
    )
```

```python
import functools
import math

import jax
import jax.numpy as jnp
from jax import lax
from jax.experimental import pallas as pl
from jax.experimental.pallas import tpu as pltpu
from jax.sharding import Mesh
from jax.sharding import PartitionSpec as P

HEAD_DIM = 128
SEQ_LEN = 4096
EPSILON = 1e-06
ALL = ("x", "core", "z", "y")
GROUP = ("x", "core", "y")
F32 = jnp.float32
BF16 = jnp.bfloat16


def dot_nn(a, b):
    return lax.dot_general(a, b, (((1,), (0,)), ((), ())), preferred_element_type=F32)


def dot_nt(a, b):
    return lax.dot_general(a, b, (((1,), (1,)), ((), ())), preferred_element_type=F32)


def dot_tn(a, b):
    return lax.dot_general(a, b, (((0,), (0,)), ((), ())), preferred_element_type=F32)


def swap(a, axis, step=1):
    return lax.ppermute(a, axis, [(i, i ^ step) for i in range(lax.axis_size(axis))])


def shift(a, axis, step):
    n = lax.axis_size(axis)
    return lax.ppermute(a, axis, [(i, i + step) for i in range(n) if 0 <= i + step < n])


def pick(a, index, axis):
    return lax.dynamic_index_in_dim(a, index, axis, keepdims=False)


def after(value, *others):
    return lax.optimization_barrier((value,) + others)[0]


def together(*values):
    return lax.optimization_barrier(values)


def copy_kernel(x_ref, out_ref):
    out_ref[...] = x_ref[...]


def settle(x):
    rows, cols = x.shape
    tile = 512 if cols % 512 == 0 else cols
    spec = pl.BlockSpec((rows, tile), lambda i: (0, i))
    return pl.pallas_call(
        copy_kernel,
        grid=(cols // tile,),
        in_specs=[spec],
        out_specs=spec,
        out_shape=jax.ShapeDtypeStruct(x.shape, x.dtype),
        name="settle",
    )(x)


def join_kernel(*refs):
    rows = refs[0].shape[0]
    for i, ref in enumerate(refs[:-1]):
        refs[-1][i * rows : (i + 1) * rows, :] = ref[...]


def join(pieces):
    rows, cols = pieces[0].shape
    tile = 512
    col = lambda n: pl.BlockSpec((n, tile), lambda i: (0, i))
    return pl.pallas_call(
        join_kernel,
        grid=(cols // tile,),
        in_specs=[col(rows)] * len(pieces),
        out_specs=col(rows * len(pieces)),
        out_shape=pltpu.HBM((rows * len(pieces), cols), pieces[0].dtype),
        name="join",
    )(*pieces)


def take_block(a, d, dp):
    part = a.shape[1] // 4
    return lax.dynamic_slice_in_dim(a, (dp ^ d) * part, part, 1)


def columns(acts, first, second, dp):
    return jnp.concatenate([take_block(acts, first, dp), take_block(acts, second, dp)], axis=1).T


def weight_grad_kernel(*refs, parts):
    outs = refs[len(refs) - parts :]
    total = dot_nn(refs[0][...], refs[1][...])
    if len(refs) - parts == 3:
        total = total + refs[2][...].astype(F32)
    rows = outs[0].shape[0]
    for i, out in enumerate(outs):
        out[...] = total[i * rows : (i + 1) * rows].astype(BF16)


def weight_grad(acts, grads, got=None, parts=1):
    rows, tokens = acts.shape
    cols = grads.shape[1]
    tile = 512
    col = lambda n: pl.BlockSpec((n, tile), lambda i: (0, i))
    args = (acts, grads) if got is None else (acts, grads, got)
    out = pl.pallas_call(
        functools.partial(weight_grad_kernel, parts=parts),
        grid=(cols // tile,),
        in_specs=[pl.BlockSpec(acts.shape, lambda i: (0, 0)), col(tokens), col(rows)][: len(args)],
        out_specs=[col(rows // parts)] * parts,
        out_shape=[jax.ShapeDtypeStruct((rows // parts, cols), BF16)] * parts,
        compiler_params=pltpu.CompilerParams(vmem_limit_bytes=40 << 20),
        cost_estimate=pl.CostEstimate(
            flops=2 * rows * tokens * cols,
            transcendentals=0,
            bytes_accessed=2 * (rows * tokens + tokens * cols + 2 * rows * cols),
        ),
        name="weight_grad",
    )(*args)
    return out if parts > 1 else out[0]


def by_owner(near):
    depth = lax.axis_size("z")
    return near.reshape(depth, 2, -1, near.shape[1])


def add(a, b):
    return (a.astype(F32) + b.astype(F32)).astype(BF16)


def split_y(a):
    y = lax.axis_index("y")
    return pick(a, 1 - y, a.ndim - 3), pick(a, y, a.ndim - 3)


def collect(a):
    out = lax.psum_scatter(a, "z", scatter_dimension=0, tiled=True)
    return out.reshape(out.shape[1:]).astype(F32)


def project_kernel(*refs):
    weight_ref, out_ref = refs[-2:]
    at = 0
    for x_ref in refs[:-2]:
        rows = x_ref.shape[0]
        out_ref[at : at + rows, :] = dot_nn(x_ref[...], weight_ref[...]).astype(out_ref.dtype)
        at += rows


def project(pieces, weights, first, count, kind):
    rows, width = pieces[0].shape
    tokens, cols = rows * len(pieces), count * width
    tile = 512
    return pl.pallas_call(
        project_kernel,
        grid=(cols // tile,),
        in_specs=[pl.BlockSpec((rows, width), lambda i: (0, 0))] * len(pieces)
        + [pl.BlockSpec((width, tile), lambda i: (0, first * (width // tile) + i))],
        out_specs=pl.BlockSpec((tokens, tile), lambda i: (0, i)),
        out_shape=jax.ShapeDtypeStruct((tokens, cols), kind),
        compiler_params=pltpu.CompilerParams(vmem_limit_bytes=50 << 20),
        cost_estimate=pl.CostEstimate(
            flops=2 * tokens * width * cols,
            transcendentals=0,
            bytes_accessed=2 * (tokens * width + width * cols + tokens * cols),
        ),
        name="project",
    )(*pieces, weights)


def project_back_kernel(*refs, count):
    total = None
    for i in range(count):
        term = dot_nt(refs[i][...], refs[count + i][...])
        total = term if total is None else total + term
    refs[-1][...] = total.astype(refs[-1].dtype)


def project_back(grads, weights, numbers, kind, block=0, tokens=None):
    width = grads[0].shape[1]
    tokens = tokens or grads[0].shape[0]
    tile = 512
    count = len(grads)
    weight = lambda number: pl.BlockSpec((tile, width), lambda i: (i, number))
    return pl.pallas_call(
        functools.partial(project_back_kernel, count=count),
        grid=(width // tile,),
        in_specs=[pl.BlockSpec((tokens, width), lambda i: (block, 0))] * count
        + [weight(number) for number in numbers],
        out_specs=pl.BlockSpec((tokens, tile), lambda i: (0, i)),
        out_shape=jax.ShapeDtypeStruct((tokens, width), kind),
        compiler_params=pltpu.CompilerParams(vmem_limit_bytes=58 << 20),
        cost_estimate=pl.CostEstimate(
            flops=2 * tokens * width * width * count,
            transcendentals=0,
            bytes_accessed=2 * (tokens + width) * width * count + 4 * tokens * width,
        ),
        name="project_back",
    )(*grads, *[weights] * count)


def level_spans(width, depth, natural):
    part = width // depth
    if not natural:
        return [[(level * part, part)] for level in range(depth)]
    piece = part // 4
    return [[((p * depth + level) * piece, piece) for p in range(4)] for level in range(depth)]


def feed_kernel(x_ref, cot_ref, pair_ref, down_ref, *refs, spans, summed):
    units = down_ref.shape[0]
    gate, up = None, None
    for level, pieces in enumerate(spans):
        cols = [x_ref[:, start : start + size] for start, size in pieces]
        cols = cols[0] if len(cols) == 1 else jnp.concatenate(cols, axis=1)
        first = dot_nt(pair_ref[level, :units, :], cols)
        second = dot_nt(pair_ref[level, units : 2 * units, :], cols)
        gate = first if gate is None else gate + first
        up = second if up is None else up + second
    grad_act = dot_nt(down_ref[...], cot_ref[...])
    sig = 1.0 / (1.0 + jnp.exp(-gate))
    silu = gate * sig
    act = (silu * up).astype(BF16)
    grad_gate = (grad_act * up * (sig * (1.0 + gate * (1.0 - sig)))).astype(BF16)
    grad_up = (grad_act * silu).astype(BF16)
    act_ref, hid_ref = refs[-2:] if not summed else refs[2:4]
    act_ref[...] = act
    hid_ref[:units, :] = grad_gate
    hid_ref[units:, :] = grad_up
    if summed:
        grad_got, grad_ref = refs[0], refs[8]
    else:
        grad_ref = refs[1]
    out_ref = refs[1 if summed else 0]
    out_ref[...] = dot_tn(act, down_ref[...]).astype(BF16)
    for level, pieces in enumerate(spans):
        both = dot_tn(grad_gate, pair_ref[level, :units, :])
        both = both + dot_tn(grad_up, pair_ref[level, units : 2 * units, :])
        at = 0
        for start, size in pieces:
            term = both[:, at : at + size]
            if summed:
                term = term + grad_got[:, start : start + size].astype(F32)
            grad_ref[:, start : start + size] = term.astype(grad_ref.dtype)
            at += size
    if summed:
        step = pl.program_id(0)
        half = grad_ref.shape[1] // 2
        for number, (mine, cols) in enumerate(
            (
                (step % 2 == 0, slice(0, half)),
                (step % 2 == 1, slice(0, half)),
                (step < 2, slice(half, 2 * half)),
                (step >= 2, slice(half, 2 * half)),
            )
        ):

            @pl.when(mine)
            def _(piece=refs[4 + number], cols=cols):
                piece[0] = grad_ref[:, cols].astype(BF16)


def feed(x, cot, pair, down, natural, got=None):
    tokens, width = x.shape
    depth, units = pair.shape[0], down.shape[0]
    units2 = 2 * units
    tile = tokens // 4
    half = width // 2
    summed = got is not None
    row = lambda n: pl.BlockSpec((tile, n), lambda i: (i, 0))
    col = lambda n: pl.BlockSpec((n, tile), lambda i: (0, i))
    piece = lambda at: pl.BlockSpec((1, tile, half), lambda i: (at(i), 0, 0))
    pieces = [
        piece(lambda i: i // 2),
        piece(lambda i: i // 2),
        piece(lambda i: jnp.minimum(i, 1)),
        piece(lambda i: jnp.maximum(i - 2, 0)),
    ]
    big = [jax.ShapeDtypeStruct((tokens, width), BF16)] * 2
    sums = [jax.ShapeDtypeStruct((2, tile, half), BF16)] * 4
    acts = [
        jax.ShapeDtypeStruct((units, tokens), BF16),
        jax.ShapeDtypeStruct((units2, tokens), BF16),
    ]
    acts_specs = [col(units), col(units2)]
    return pl.pallas_call(
        functools.partial(
            feed_kernel, spans=level_spans(width, depth, natural), summed=summed
        ),
        grid=(4,),
        in_specs=[
            row(width),
            row(width),
            pl.BlockSpec(pair.shape, lambda i: (0, 0, 0)),
            pl.BlockSpec(down.shape, lambda i: (0, 0)),
        ]
        + ([row(width)] if summed else []),
        out_specs=[row(width)] + (acts_specs + pieces if summed else [row(width)] + acts_specs),
        out_shape=big[:1] + acts + sums if summed else big + acts,
        scratch_shapes=[pltpu.VMEM((tile, width), F32)] if summed else [],
        compiler_params=pltpu.CompilerParams(vmem_limit_bytes=56 << 20),
        cost_estimate=pl.CostEstimate(
            flops=12 * tokens * width * units,
            transcendentals=tokens * units,
            bytes_accessed=2 * (4 * tokens * width + 3 * units * width + 3 * units * tokens),
        ),
        name="feed_sum" if summed else "feed",
    )(x, cot, pair, down, *((got,) if summed else ()))


def feed_weights_kernel(*refs, count):
    pair_ref, down_ref = refs[4 * count :]
    pair, down = None, None
    for i in range(count):
        x_ref, cot_ref, act_ref, hid_ref = refs[4 * i : 4 * i + 4]
        first = dot_nn(hid_ref[...], x_ref[...])
        second = dot_nn(act_ref[...], cot_ref[...])
        pair = first if pair is None else pair + first
        down = second if down is None else down + second
    pair, down = pair.astype(BF16), down.astype(BF16)
    for level in range(pair_ref.shape[0]):
        size = pair_ref.shape[2]
        pair_ref[level] = pair[:, level * size : (level + 1) * size]
    for level in range(down_ref.shape[0]):
        size = down_ref.shape[1]
        down_ref[level] = down[level * size : (level + 1) * size]


def feed_weights(sets, depth, natural):
    x, _, act, hid = sets[0]
    tokens, width = x.shape
    units, units2 = act.shape[0], hid.shape[0]
    steps = 4 if natural else depth
    part = width // steps
    if natural:
        pair_spec = pl.BlockSpec((depth, units2, part // depth), lambda i: (0, 0, i))
    else:
        pair_spec = pl.BlockSpec((1, units2, part), lambda i: (i, 0, 0))
    return pl.pallas_call(
        functools.partial(feed_weights_kernel, count=len(sets)),
        grid=(steps,),
        in_specs=[
            pl.BlockSpec((tokens, part), lambda i: (0, i)),
            pl.BlockSpec((tokens, part), lambda i: (0, i)),
            pl.BlockSpec(act.shape, lambda i: (0, 0)),
            pl.BlockSpec(hid.shape, lambda i: (0, 0)),
        ]
        * len(sets),
        out_specs=[
            pair_spec,
            pl.BlockSpec((depth, units // depth, part), lambda i: (0, 0, i)),
        ],
        out_shape=[
            pltpu.HBM((depth, units2, width // depth), BF16),
            pltpu.HBM((depth, units // depth, width), BF16),
        ],
        compiler_params=pltpu.CompilerParams(vmem_limit_bytes=50 << 20),
        cost_estimate=pl.CostEstimate(
            flops=6 * tokens * width * units * len(sets),
            transcendentals=0,
            bytes_accessed=2 * (2 * tokens * width + 3 * units * tokens) * len(sets)
            + 6 * units * width,
        ),
        name="feed_weights",
    )(*[v for group in sets for v in group])


def reduce_last(first, first_y, second, second_x):
    first, second = add(first, first_y), add(second, second_x)
    return first[0], first[1], second[0], second[1]


def reduce_done(first, first_x, second, second_y):
    first = first.astype(F32) + first_x.astype(F32)
    second = second.astype(F32) + second_y.astype(F32)
    return jnp.concatenate([first, second], axis=-1)


LOG2E = 1.4426950408889634


def write_bias(query_ref, key_ref, bias_ref):
    query_code = query_ref[:, 0:1]
    query_pos = query_ref[:, 1:2]
    key_code = key_ref[0:1, :]
    key_pos = key_ref[1:2, :]
    key_valid = key_ref[2:3, :]
    allowed = (
        (query_code == key_code)
        & (key_pos <= query_pos)
        & ((key_valid == 1) | (key_pos == query_pos))
    )
    bias_ref[...] = jnp.where(allowed, 0.0, -1e30)


def forward_kernel(query_ref, key_ref, q_ref, k_ref, v_ref, out_ref, low_ref, bias_ref, *, scale):
    @pl.when(pl.program_id(0) == 0)
    def _():
        write_bias(query_ref, key_ref, bias_ref)

    scores = dot_nt(q_ref[...], k_ref[...])
    weights = jnp.exp2(scores * (scale * LOG2E) + bias_ref[...])
    totals = jnp.sum(weights, axis=-1, keepdims=True)
    unnorm = dot_nn(weights.astype(BF16), v_ref[...])
    attended = unnorm / totals
    out_ref[...] = attended
    low_ref[...] = attended.astype(BF16)


def backward_kernel(
    query_ref, key_ref, q_ref, k_ref, v_ref, att_ref, grad_ref, dq_ref, dk_ref, dv_ref, bias_ref, *, scale
):
    @pl.when(pl.program_id(0) == 0)
    def _():
        write_bias(query_ref, key_ref, bias_ref)

    q, k, v = q_ref[...], k_ref[...], v_ref[...]
    grad = grad_ref[...]
    scores = dot_nt(q, k)
    weights = jnp.exp2(scores * (scale * LOG2E) + bias_ref[...])
    totals = jnp.sum(weights, axis=-1, keepdims=True)
    grad_totals = -jnp.sum(grad * att_ref[...], axis=-1, keepdims=True) / totals
    grad_unnorm = (grad / totals).astype(BF16)
    grad_weights = dot_nt(grad_unnorm, v)
    grad_scores = (weights * (grad_weights + grad_totals)).astype(BF16)
    dq_ref[...] = (dot_nn(grad_scores, k) * scale).astype(BF16)
    dk_ref[...] = (dot_tn(grad_scores, q) * scale).astype(BF16)
    dv_ref[...] = dot_tn(weights.astype(BF16), grad_unnorm).astype(BF16)


def attention_specs(rows, keys):
    whole = lambda shape: pl.BlockSpec(shape, lambda h: (0, 0))
    head = lambda n, first=0: pl.BlockSpec((n, HEAD_DIM), lambda h: (0, first + h))
    return whole, head


def attend_forward(query_info, key_info, queries, pairs):
    rows, width = queries.shape
    count = pairs.shape[0]
    whole, head = attention_specs(rows, count)
    return pl.pallas_call(
        functools.partial(forward_kernel, scale=1.0 / math.sqrt(HEAD_DIM)),
        grid=(width // HEAD_DIM,),
        in_specs=[
            whole(query_info.shape),
            whole(key_info.shape),
            head(rows),
            head(count),
            head(count, width // HEAD_DIM),
        ],
        out_specs=[head(rows), head(rows)],
        out_shape=[
            jax.ShapeDtypeStruct((rows, width), F32),
            jax.ShapeDtypeStruct((rows, width), BF16),
        ],
        scratch_shapes=[pltpu.VMEM((rows, count), F32)],
        compiler_params=pltpu.CompilerParams(vmem_limit_bytes=40 << 20),
        cost_estimate=pl.CostEstimate(
            flops=4 * rows * count * width,
            transcendentals=rows * count * width // HEAD_DIM,
            bytes_accessed=2 * (2 * count + 4 * rows) * width,
        ),
        name="attend_forward",
    )(query_info, key_info, queries, pairs, pairs)


def attend_backward(query_info, key_info, queries, pairs, attended, grads):
    rows, width = queries.shape
    count = pairs.shape[0]
    whole, head = attention_specs(rows, count)
    return pl.pallas_call(
        functools.partial(backward_kernel, scale=1.0 / math.sqrt(HEAD_DIM)),
        grid=(width // HEAD_DIM,),
        in_specs=[
            whole(query_info.shape),
            whole(key_info.shape),
            head(rows),
            head(count),
            head(count, width // HEAD_DIM),
            head(rows),
            head(rows),
        ],
        out_specs=[head(rows), head(count), head(count)],
        out_shape=[
            jax.ShapeDtypeStruct((rows, width), BF16),
            jax.ShapeDtypeStruct((count, width), BF16),
            jax.ShapeDtypeStruct((count, width), BF16),
        ],
        scratch_shapes=[pltpu.VMEM((rows, count), F32)],
        compiler_params=pltpu.CompilerParams(vmem_limit_bytes=48 << 20),
        cost_estimate=pl.CostEstimate(
            flops=10 * rows * count * width,
            transcendentals=rows * count * width // HEAD_DIM,
            bytes_accessed=2 * (4 * count + 6 * rows) * width,
        ),
        name="attend_backward",
    )(query_info, key_info, queries, pairs, pairs, attended, grads)


def shards(
    inputs,
    kv_input,
    segment_ids,
    valid_mask,
    w_query,
    w_key,
    w_value,
    w_out,
    w_gate,
    w_up,
    w_down,
    gain_attn,
    gain_ffn,
    cotangent,
):
    rows, width = inputs.shape
    x, core, z, y = (lax.axis_index(name) for name in ALL)
    depth = lax.axis_size("z")
    devices = 4 * depth * 2
    dp, fsdp = x * 2 + core, z * 2 + y
    group_rows = rows * depth * 2
    seq_length = min(SEQ_LEN, group_rows)
    wide = w_query.shape[0]
    hidden = w_down.shape[0]

    small = jnp.concatenate(
        [gain_attn.astype(F32), gain_ffn.astype(F32), segment_ids.astype(F32), valid_mask.astype(F32)]
    )
    small = lax.all_to_all(
        jnp.broadcast_to(small[None], (devices, small.shape[0])), ALL, 0, 0, tiled=True
    )
    reach = min(-(-(seq_length // 2 - 1) // (2 * rows)), depth - 1)
    natural = 2 * wide % 128 == 0


    weights = jnp.concatenate([w_key, w_value, w_query, w_out], axis=1)
    weights = lax.all_gather(weights, ALL, axis=0, tiled=True)
    levels = [kv_input, shift(kv_input, "z", 1)]
    others = [swap(kv_input, "y")]
    cot_y = swap(cotangent, "y")

    def split_columns(w):
        return w.reshape(wide, 4, depth, 2, hidden).transpose(1, 3, 0, 2, 4)

    pair = jnp.stack([split_columns(w_gate), split_columns(w_up)], axis=2)
    pair = pair.reshape(8, 2 * wide, depth * hidden)
    levels[1], others[0], pair, cot_y = together(levels[1], others[0], pair, cot_y)

    others.append(swap(levels[1], "y"))
    for _ in range(reach - 1):
        levels.append(shift(levels[-1], "z", 1))
    for level in levels[2:-1]:
        others.append(swap(level, "y"))
    pair = lax.all_to_all(pair, GROUP, 0, 0, tiled=True)
    cot_pair = jnp.concatenate([cotangent, cot_y])
    pair, cot_pair, *held = together(pair, cot_pair, *others, *levels[1:])
    others, levels = held[: len(others)], [kv_input] + held[len(others) :]

    if len(others) < len(levels):
        others.append(swap(levels[-1], "y"))
    pair = pair.reshape(8, 2, wide, depth * hidden).transpose(1, 3, 0, 2)
    pair = settle(pair.reshape(2 * depth * hidden, 8 * wide))
    *held, pair, small = together(*levels, *others, pair, small)
    halo = join([held[i + j] for i in range(reach + 1) for j in (0, reach + 1)])
    halo_far, halo_near = columns(halo, 1, 3, dp), columns(halo, 0, 2, dp)
    full_gain_attn = small[:, :wide].reshape(-1)
    full_gain_ffn = small[:, wide : 2 * wide].reshape(-1)
    ids_all = lax.dynamic_slice_in_dim(small, dp * depth * 2, depth * 2, 0)[:, 2 * wide :]
    ids_all = ids_all.astype(jnp.int32)
    block_ids = []
    for level in range(reach + 1):
        for other in range(2):
            block_ids.append(2 * (z - level) + (y ^ other))
    key_pos, key_seg, key_valid = [], [], []
    for block in block_ids:
        here = pick(ids_all, jnp.maximum(block, 0), 0)
        key_seg.append(here[:rows])
        key_valid.append(here[rows:])
        key_pos.append(block * rows + jnp.arange(rows, dtype=jnp.int32))
    key_pos, key_seg, key_valid = (jnp.concatenate(v) for v in (key_pos, key_seg, key_valid))
    query_pos = fsdp * rows + jnp.arange(rows, dtype=jnp.int32)
    code = lambda seg, pos: seg * 4096 + pos // seq_length
    zeros = jnp.zeros_like(key_pos)
    key_info = jnp.stack([code(key_seg, key_pos), key_pos, key_valid] + [zeros] * 5)
    zeros = jnp.zeros_like(query_pos)
    query_info = jnp.stack([code(segment_ids, query_pos), query_pos] + [zeros] * 6, axis=1)
    stream = inputs.astype(F32)
    squares_in = jnp.sum(stream * stream, axis=-1, keepdims=True)
    factor_one = lax.rsqrt(squares_in / width + EPSILON)
    unit_one = stream * factor_one
    normed1 = (unit_one * full_gain_attn).astype(BF16)
    normed1_far, normed1_near = columns(normed1, 1, 3, dp), columns(normed1, 0, 2, dp)
    (
        pair, weights, cot_pair, down, halo, halo_far, halo_near, full_gain_ffn, normed1, normed1_far,
        normed1_near, query_info, key_info,
    ) = together(
        pair, weights, cot_pair, w_down, halo, halo_far, halo_near, full_gain_ffn, normed1,
        normed1_far, normed1_near, query_info, key_info,
    )

    pair = lax.all_gather(pair, "z", axis=0, tiled=False)
    cot_x = swap(cot_pair, "x")
    pairs = project([halo], weights, 0, 2, BF16)
    cot_x, pairs = together(cot_x, pairs)
    queries = project([normed1], weights, 2, 1, BF16)
    attended_f, attended = attend_forward(query_info, key_info, queries, pairs)
    middle = stream + project([attended], weights, 3, 1, F32)
    squares_mid = jnp.sum(middle * middle, axis=-1, keepdims=True)
    factor_two = lax.rsqrt(squares_mid / width + EPSILON)
    unit_two = middle * factor_two
    normed2 = (unit_two * full_gain_ffn).astype(BF16)
    if not natural:
        normed2 = normed2.reshape(rows, 4, depth, 2 * wide).swapaxes(1, 2).reshape(rows, width)
    half = width // 2
    first, second, cot_x = together(normed2[:, :half], normed2[:, half:], cot_x)
    cot_near = jnp.concatenate([cot_pair, cot_x])
    cot_far = swap(cot_near, "core")

    first_x, second_y = swap(first, "x"), swap(second, "y")
    first_x, second_y, cot_near, cot_far, pair, down = together(
        first_x, second_y, cot_near, cot_far, pair, down
    )
    part_down = lax.all_gather(down, "z", axis=0, tiled=False)
    first, second = jnp.stack([first, first_x]), jnp.stack([second, second_y])
    first_y, second_x = swap(first, "y"), swap(second, "x")
    attended_far, attended_near = columns(attended, 1, 3, dp), columns(attended, 0, 2, dp)
    first_y, second_x, attended_far, attended_near = together(
        first_y, second_x, attended_far, attended_near
    )
    first = jnp.stack([first, first_y], axis=1)
    second = jnp.stack([second, second_x])
    x_near = jnp.concatenate([first, second], axis=-1).reshape(4 * rows, width)
    x_far = swap(x_near, "core")
    feeds = pair
    part_down = part_down.reshape(depth * hidden, width)

    out_far, grad_far, act_far, hid_far = feed(x_far, cot_far, feeds, part_down, natural)
    got = swap(grad_far, "core")
    out_near, act_near, hid_near, first, first_away, second, second_away = feed(
        x_near, cot_near, feeds, part_down, natural, got
    )
    out_got = swap(out_far, "core")
    first_y, second_x = swap(first_away, "y"), swap(second_away, "x")
    grad_pair, grad_down = feed_weights(
        [(x_near, cot_near, act_near, hid_near), (x_far, cot_far, act_far, hid_far)], depth, natural
    )
    first, first_away, second, second_away = reduce_last(first, first_y, second, second_x)
    first, first_away, second, second_away, grad_pair, grad_down, out_near, out_got = together(
        first, first_away, second, second_away, grad_pair, grad_down, out_near, out_got
    )
    grad_pair = lax.psum_scatter(grad_pair, "z", scatter_dimension=0, tiled=True)
    grad_down = lax.psum_scatter(grad_down, "z", scatter_dimension=0, tiled=True)
    first_x, second_y = swap(first_away, "x"), swap(second_away, "y")
    grad_normed2 = reduce_done(first, first_x, second, second_y)
    if not natural:
        grad_normed2 = grad_normed2.reshape(rows, depth, 4, 2 * wide).swapaxes(1, 2)
        grad_normed2 = grad_normed2.reshape(rows, width)

    part_gain_ffn = jnp.sum(grad_normed2 * unit_two, axis=0)
    inner = grad_normed2 * full_gain_ffn
    grad_middle = cotangent.astype(F32) + factor_two * (
        inner - unit_two * jnp.mean(inner * unit_two, axis=-1, keepdims=True)
    )
    grad_branch = grad_middle.astype(BF16)
    far_out = weight_grad(attended_far, grad_branch)
    far_out, grad_branch, grad_middle = together(far_out, grad_branch, grad_middle)
    got_out = swap(far_out, "core")
    grad_attended = project_back([grad_branch], weights, [3], F32)
    out_home, out_away = weight_grad(attended_near, grad_branch, got_out, 2)
    out_home, out_away, grad_attended = together(out_home, out_away, grad_attended)

    out_x = swap(out_away, "x")
    grad_queries, grad_keys, grad_values = attend_backward(
        query_info, key_info, queries, pairs, attended_f, grad_attended
    )
    far_key = weight_grad(halo_far, grad_keys)
    out_x, far_key, grad_keys, grad_values, grad_queries = together(
        out_x, far_key, grad_keys, grad_values, grad_queries
    )

    got_key = swap(far_key, "core")
    far_value = weight_grad(halo_far, grad_values)
    got_key, far_value, grad_keys, grad_values, grad_queries, grad_pair = together(
        got_key, far_value, grad_keys, grad_values, grad_queries, grad_pair
    )

    got_value = swap(far_value, "core")
    key_home, key_away = weight_grad(halo_near, grad_keys, got_key, 2)
    far_query = weight_grad(normed1_far, grad_queries)
    got_value, key_home, key_away, far_query, grad_keys, grad_values, grad_queries = together(
        got_value, key_home, key_away, far_query, grad_keys, grad_values, grad_queries
    )

    got_query = swap(far_query, "core")
    value_near = weight_grad(halo_near, grad_values, got_value)
    out_away, out_home = split_y(by_owner(add(out_home, out_x)))
    got_query, value_near, key_away, out_away, out_home, grad_keys, grad_values = together(
        got_query, value_near, key_away, out_away, out_home, grad_keys, grad_values
    )

    key_x = swap(key_away, "x")
    value_away, value_home = split_y(value_near.reshape(2, depth, 2, wide, width))
    value_y = swap(value_away, "y")
    grad_pair = settle(settle(grad_pair.reshape(2 * depth * hidden, 8 * wide)).T)
    grad_pair = grad_pair.reshape(8, wide, 2 * depth * hidden)
    grad_pair = lax.all_to_all(grad_pair, GROUP, 0, 0, tiled=True)
    halves = [grad_keys, grad_values]
    back = project_back(halves, weights, [0, 1], BF16, reach, 2 * rows)
    back = shift(back, "z", -1)
    grad_halo = project_back(halves, weights, [0, 1], BF16, 0, reach * 2 * rows)
    query_home, query_away = weight_grad(normed1_near, grad_queries, got_query, 2)
    key_x, value_y, query_home, query_away, grad_halo, back, grad_queries, *held = together(
        key_x, value_y, query_home, query_away, grad_halo, back, grad_queries, grad_pair, out_near, out_got,
        grad_down,
    )
    grad_pair, out_near, out_got, grad_down = held
    share_down = grad_down.reshape(hidden, width).astype(F32)

    key_away, key_home = split_y(by_owner(add(key_home, key_x)))
    query_x, key_y, out_y = swap(query_away, "x"), swap(key_away, "y"), swap(out_away, "y")
    for level in reversed(range(1, reach)):
        at = level * 2 * rows
        back = shift(add(grad_halo[at : at + 2 * rows], back), "z", -1)
    grad_normed1 = project_back([grad_queries], weights, [2], F32)
    value_home = add(value_home, value_y)
    sums = add(out_near, out_got).reshape(2, 2, rows, width)
    sums = sums[:, 0, :, :half], sums[:, 1, :, :half], sums[0, :, :, half:], sums[1, :, :, half:]
    query_x, key_y, out_y, back, grad_normed1, grad_pair, value_home, *sums = together(
        query_x, key_y, out_y, back, grad_normed1, grad_pair, value_home, *sums
    )

    shares_first = jnp.concatenate([add(key_home, key_y), add(out_home, out_y)], axis=1)
    shares_first = lax.psum_scatter(shares_first, "z", scatter_dimension=0, tiled=True)
    query_away, query_home = split_y(by_owner(add(query_home, query_x)))
    query_y, value_x = swap(query_away, "y"), swap(value_home[1], "x")
    sum_y, sum_x = swap(sums[1], "y"), swap(sums[3], "x")
    back = add(grad_halo[: 2 * rows], back)
    grad_pair = grad_pair.reshape(4, 2, wide, 2, depth, hidden).transpose(3, 2, 0, 4, 1, 5)
    grad_pair = grad_pair.reshape(2, wide, devices * hidden).astype(F32)
    part_gain_attn = jnp.sum(grad_normed1 * unit_one, axis=0)
    inner = grad_normed1 * full_gain_attn
    grad_inputs = grad_middle + factor_one * (
        inner - unit_one * jnp.mean(inner * unit_one, axis=-1, keepdims=True)
    )
    query_y, value_x, back, sum_y, sum_x, share_gate, share_up, grad_inputs = together(
        query_y, value_x, back, sum_y, sum_x, grad_pair[0], grad_pair[1], grad_inputs
    )

    shares = jnp.concatenate([add(value_home[0], value_x), add(query_home, query_y)], axis=1)
    shares = lax.psum_scatter(shares, "z", scatter_dimension=0, tiled=True)
    sums = reduce_last(sums[0], sum_y, sums[2], sum_x)
    sum_x, sum_y, back_y = swap(sums[1], "x"), swap(sums[3], "y"), swap(back[rows:], "y")
    sum_x, sum_y = together(sum_x, sum_y)
    grad_kv_input = back[:rows].astype(F32) + back_y.astype(F32)
    result = middle + reduce_done(sums[0], sum_x, sums[2], sum_y)
    valid = valid_mask.astype(F32)
    squares_out = jnp.sum(result * result, axis=-1)
    sums = jnp.stack(
        [
            jnp.sum(valid * squares_in[:, 0]),
            jnp.sum(valid * squares_mid[:, 0]),
            jnp.sum(valid * squares_out),
            jnp.sum(valid),
        ]
    )
    tiny = jnp.concatenate(
        [
            part_gain_attn.reshape(devices, wide),
            part_gain_ffn.reshape(devices, wide),
            jnp.broadcast_to(sums[None], (devices, 4)),
        ],
        axis=1,
    )
    tiny = lax.all_to_all(tiny, ALL, 0, 0, tiled=True)
    share_key, share_out = shares_first[0, :wide].astype(F32), shares_first[0, wide:].astype(F32)
    share_value, share_query = shares[0, :wide].astype(F32), shares[0, wide:].astype(F32)

    tiny = jnp.sum(tiny, axis=0)
    divisor = tiny[2 * wide + 3] * width
    rms_in = jnp.sqrt(tiny[2 * wide] / divisor)
    rms_mid = jnp.sqrt(tiny[2 * wide + 1] / divisor)
    rms_out = jnp.sqrt(tiny[2 * wide + 2] / divisor)
    return (
        result.astype(BF16),
        grad_inputs,
        grad_kv_input,
        share_query,
        share_key,
        share_value,
        share_out,
        share_gate,
        share_up,
        share_down,
        tiny[:wide],
        tiny[wide : 2 * wide],
        rms_in,
        rms_mid,
        rms_out,
    )


def solution(mesh):
    inner = Mesh(
        mesh.devices.reshape(2, mesh.shape["dp"] // 2, mesh.shape["fsdp"] // 2, 2), ALL
    )
    rows, flat = P(ALL, None), P(ALL)
    return jax.shard_map(
        shards,
        mesh=inner,
        in_specs=(rows, rows, flat, flat) + (rows,) * 7 + (flat, flat, rows),
        out_specs=(rows,) * 10 + (flat, flat, P(), P(), P()),
        check_vma=False,
    )
```

```python
import functools
import math

import jax
import jax.numpy as jnp
from jax import lax
from jax.experimental import pallas as pl
from jax.experimental.pallas import tpu as pltpu
from jax.sharding import Mesh
from jax.sharding import PartitionSpec as P

HEAD_DIM = 128
SEQ_LEN = 4096
EPSILON = 1e-06
ALL = ("x", "core", "z", "y")
GROUP = ("x", "core", "y")
F32 = jnp.float32
BF16 = jnp.bfloat16


def dot_nn(a, b):
    return lax.dot_general(a, b, (((1,), (0,)), ((), ())), preferred_element_type=F32)


def dot_nt(a, b):
    return lax.dot_general(a, b, (((1,), (1,)), ((), ())), preferred_element_type=F32)


def dot_tn(a, b):
    return lax.dot_general(a, b, (((0,), (0,)), ((), ())), preferred_element_type=F32)


def swap(a, axis, step=1):
    return lax.ppermute(a, axis, [(i, i ^ step) for i in range(lax.axis_size(axis))])


def shift(a, axis, step):
    n = lax.axis_size(axis)
    return lax.ppermute(a, axis, [(i, i + step) for i in range(n) if 0 <= i + step < n])


def pick(a, index, axis):
    return lax.dynamic_index_in_dim(a, index, axis, keepdims=False)


def after(value, *others):
    return lax.optimization_barrier((value,) + others)[0]


def together(*values):
    return lax.optimization_barrier(values)


def copy_kernel(x_ref, out_ref):
    out_ref[...] = x_ref[...]


def settle(x):
    rows, cols = x.shape
    tile = 512 if cols % 512 == 0 else cols
    spec = pl.BlockSpec((rows, tile), lambda i: (0, i))
    return pl.pallas_call(
        copy_kernel,
        grid=(cols // tile,),
        in_specs=[spec],
        out_specs=spec,
        out_shape=jax.ShapeDtypeStruct(x.shape, x.dtype),
        name="settle",
    )(x)


def join_kernel(*refs):
    rows = refs[0].shape[0]
    for i, ref in enumerate(refs[:-1]):
        refs[-1][i * rows : (i + 1) * rows, :] = ref[...]


def join(pieces):
    rows, cols = pieces[0].shape
    tile = 512
    col = lambda n: pl.BlockSpec((n, tile), lambda i: (0, i))
    return pl.pallas_call(
        join_kernel,
        grid=(cols // tile,),
        in_specs=[col(rows)] * len(pieces),
        out_specs=col(rows * len(pieces)),
        out_shape=pltpu.HBM((rows * len(pieces), cols), pieces[0].dtype),
        name="join",
    )(*pieces)


def take_block(a, d, dp):
    part = a.shape[1] // 4
    return lax.dynamic_slice_in_dim(a, (dp ^ d) * part, part, 1)


def columns(acts, first, second, dp):
    return jnp.concatenate([take_block(acts, first, dp), take_block(acts, second, dp)], axis=1).T


def weight_grad_kernel(*refs, parts):
    outs = refs[len(refs) - parts :]
    total = dot_nn(refs[0][...], refs[1][...])
    if len(refs) - parts == 3:
        total = total + refs[2][...].astype(F32)
    rows = outs[0].shape[0]
    for i, out in enumerate(outs):
        out[...] = total[i * rows : (i + 1) * rows].astype(BF16)


def weight_grad(acts, grads, got=None, parts=1):
    rows, tokens = acts.shape
    cols = grads.shape[1]
    tile = 512
    col = lambda n: pl.BlockSpec((n, tile), lambda i: (0, i))
    args = (acts, grads) if got is None else (acts, grads, got)
    out = pl.pallas_call(
        functools.partial(weight_grad_kernel, parts=parts),
        grid=(cols // tile,),
        in_specs=[pl.BlockSpec(acts.shape, lambda i: (0, 0)), col(tokens), col(rows)][: len(args)],
        out_specs=[col(rows // parts)] * parts,
        out_shape=[jax.ShapeDtypeStruct((rows // parts, cols), BF16)] * parts,
        compiler_params=pltpu.CompilerParams(vmem_limit_bytes=40 << 20),
        cost_estimate=pl.CostEstimate(
            flops=2 * rows * tokens * cols,
            transcendentals=0,
            bytes_accessed=2 * (rows * tokens + tokens * cols + 2 * rows * cols),
        ),
        name="weight_grad",
    )(*args)
    return out if parts > 1 else out[0]


def by_owner(near):
    depth = lax.axis_size("z")
    return near.reshape(depth, 2, -1, near.shape[1])


def add(a, b):
    return (a.astype(F32) + b.astype(F32)).astype(BF16)


def split_y(a):
    y = lax.axis_index("y")
    return pick(a, 1 - y, a.ndim - 3), pick(a, y, a.ndim - 3)


def collect(a):
    out = lax.psum_scatter(a, "z", scatter_dimension=0, tiled=True)
    return out.reshape(out.shape[1:]).astype(F32)


def project_kernel(*refs):
    weight_ref, out_ref = refs[-2:]
    at = 0
    for x_ref in refs[:-2]:
        rows = x_ref.shape[0]
        out_ref[at : at + rows, :] = dot_nn(x_ref[...], weight_ref[...]).astype(out_ref.dtype)
        at += rows


def project(pieces, weights, first, count, kind):
    rows, width = pieces[0].shape
    tokens, cols = rows * len(pieces), count * width
    tile = 512
    return pl.pallas_call(
        project_kernel,
        grid=(cols // tile,),
        in_specs=[pl.BlockSpec((rows, width), lambda i: (0, 0))] * len(pieces)
        + [pl.BlockSpec((width, tile), lambda i: (0, first * (width // tile) + i))],
        out_specs=pl.BlockSpec((tokens, tile), lambda i: (0, i)),
        out_shape=jax.ShapeDtypeStruct((tokens, cols), kind),
        compiler_params=pltpu.CompilerParams(vmem_limit_bytes=50 << 20),
        cost_estimate=pl.CostEstimate(
            flops=2 * tokens * width * cols,
            transcendentals=0,
            bytes_accessed=2 * (tokens * width + width * cols + tokens * cols),
        ),
        name="project",
    )(*pieces, weights)


def project_back_kernel(*refs, count):
    total = None
    for i in range(count):
        term = dot_nt(refs[i][...], refs[count + i][...])
        total = term if total is None else total + term
    refs[-1][...] = total.astype(refs[-1].dtype)


def project_back(grads, weights, numbers, kind, block=0, tokens=None):
    width = grads[0].shape[1]
    tokens = tokens or grads[0].shape[0]
    tile = 512
    count = len(grads)
    weight = lambda number: pl.BlockSpec((tile, width), lambda i: (i, number))
    return pl.pallas_call(
        functools.partial(project_back_kernel, count=count),
        grid=(width // tile,),
        in_specs=[pl.BlockSpec((tokens, width), lambda i: (block, 0))] * count
        + [weight(number) for number in numbers],
        out_specs=pl.BlockSpec((tokens, tile), lambda i: (0, i)),
        out_shape=jax.ShapeDtypeStruct((tokens, width), kind),
        compiler_params=pltpu.CompilerParams(vmem_limit_bytes=58 << 20),
        cost_estimate=pl.CostEstimate(
            flops=2 * tokens * width * width * count,
            transcendentals=0,
            bytes_accessed=2 * (tokens + width) * width * count + 4 * tokens * width,
        ),
        name="project_back",
    )(*grads, *[weights] * count)


def level_spans(width, depth, natural):
    part = width // depth
    if not natural:
        return [[(level * part, part)] for level in range(depth)]
    piece = part // 4
    return [[((p * depth + level) * piece, piece) for p in range(4)] for level in range(depth)]


def feed_kernel(x_ref, cot_ref, pair_ref, down_ref, *refs, spans, summed):
    units = down_ref.shape[0]
    gate, up = None, None
    for level, pieces in enumerate(spans):
        cols = [x_ref[:, start : start + size] for start, size in pieces]
        cols = cols[0] if len(cols) == 1 else jnp.concatenate(cols, axis=1)
        first = dot_nt(pair_ref[level, :units, :], cols)
        second = dot_nt(pair_ref[level, units : 2 * units, :], cols)
        gate = first if gate is None else gate + first
        up = second if up is None else up + second
    grad_act = dot_nt(down_ref[...], cot_ref[...])
    sig = 1.0 / (1.0 + jnp.exp(-gate))
    silu = gate * sig
    act = (silu * up).astype(BF16)
    grad_gate = (grad_act * up * (sig * (1.0 + gate * (1.0 - sig)))).astype(BF16)
    grad_up = (grad_act * silu).astype(BF16)
    act_ref, hid_ref = refs[-2:] if not summed else refs[2:4]
    act_ref[...] = act
    hid_ref[:units, :] = grad_gate
    hid_ref[units:, :] = grad_up
    if summed:
        grad_got, grad_ref = refs[0], refs[8]
    else:
        grad_ref = refs[1]
    out_ref = refs[1 if summed else 0]
    out_ref[...] = dot_tn(act, down_ref[...]).astype(BF16)
    for level, pieces in enumerate(spans):
        both = dot_tn(grad_gate, pair_ref[level, :units, :])
        both = both + dot_tn(grad_up, pair_ref[level, units : 2 * units, :])
        at = 0
        for start, size in pieces:
            term = both[:, at : at + size]
            if summed:
                term = term + grad_got[:, start : start + size].astype(F32)
            grad_ref[:, start : start + size] = term.astype(grad_ref.dtype)
            at += size
    if summed:
        step = pl.program_id(0)
        half = grad_ref.shape[1] // 2
        for number, (mine, cols) in enumerate(
            (
                (step % 2 == 0, slice(0, half)),
                (step % 2 == 1, slice(0, half)),
                (step < 2, slice(half, 2 * half)),
                (step >= 2, slice(half, 2 * half)),
            )
        ):

            @pl.when(mine)
            def _(piece=refs[4 + number], cols=cols):
                piece[0] = grad_ref[:, cols].astype(BF16)


def feed(x, cot, pair, down, natural, got=None):
    tokens, width = x.shape
    depth, units = pair.shape[0], down.shape[0]
    units2 = 2 * units
    tile = tokens // 4
    half = width // 2
    summed = got is not None
    row = lambda n: pl.BlockSpec((tile, n), lambda i: (i, 0))
    col = lambda n: pl.BlockSpec((n, tile), lambda i: (0, i))
    piece = lambda at: pl.BlockSpec((1, tile, half), lambda i: (at(i), 0, 0))
    pieces = [
        piece(lambda i: i // 2),
        piece(lambda i: i // 2),
        piece(lambda i: jnp.minimum(i, 1)),
        piece(lambda i: jnp.maximum(i - 2, 0)),
    ]
    big = [jax.ShapeDtypeStruct((tokens, width), BF16)] * 2
    sums = [jax.ShapeDtypeStruct((2, tile, half), BF16)] * 4
    acts = [
        jax.ShapeDtypeStruct((units, tokens), BF16),
        jax.ShapeDtypeStruct((units2, tokens), BF16),
    ]
    acts_specs = [col(units), col(units2)]
    return pl.pallas_call(
        functools.partial(
            feed_kernel, spans=level_spans(width, depth, natural), summed=summed
        ),
        grid=(4,),
        in_specs=[
            row(width),
            row(width),
            pl.BlockSpec(pair.shape, lambda i: (0, 0, 0)),
            pl.BlockSpec(down.shape, lambda i: (0, 0)),
        ]
        + ([row(width)] if summed else []),
        out_specs=[row(width)] + (acts_specs + pieces if summed else [row(width)] + acts_specs),
        out_shape=big[:1] + acts + sums if summed else big + acts,
        scratch_shapes=[pltpu.VMEM((tile, width), F32)] if summed else [],
        compiler_params=pltpu.CompilerParams(vmem_limit_bytes=56 << 20),
        cost_estimate=pl.CostEstimate(
            flops=12 * tokens * width * units,
            transcendentals=tokens * units,
            bytes_accessed=2 * (4 * tokens * width + 3 * units * width + 3 * units * tokens),
        ),
        name="feed_sum" if summed else "feed",
    )(x, cot, pair, down, *((got,) if summed else ()))


def feed_weights_kernel(*refs, count):
    pair_ref, down_ref = refs[4 * count :]
    pair, down = None, None
    for i in range(count):
        x_ref, cot_ref, act_ref, hid_ref = refs[4 * i : 4 * i + 4]
        first = dot_nn(hid_ref[...], x_ref[...])
        second = dot_nn(act_ref[...], cot_ref[...])
        pair = first if pair is None else pair + first
        down = second if down is None else down + second
    pair, down = pair.astype(BF16), down.astype(BF16)
    for level in range(pair_ref.shape[0]):
        size = pair_ref.shape[2]
        pair_ref[level] = pair[:, level * size : (level + 1) * size]
    for level in range(down_ref.shape[0]):
        size = down_ref.shape[1]
        down_ref[level] = down[level * size : (level + 1) * size]


def feed_weights(sets, depth, natural):
    x, _, act, hid = sets[0]
    tokens, width = x.shape
    units, units2 = act.shape[0], hid.shape[0]
    steps = 4 if natural else depth
    part = width // steps
    if natural:
        pair_spec = pl.BlockSpec((depth, units2, part // depth), lambda i: (0, 0, i))
    else:
        pair_spec = pl.BlockSpec((1, units2, part), lambda i: (i, 0, 0))
    return pl.pallas_call(
        functools.partial(feed_weights_kernel, count=len(sets)),
        grid=(steps,),
        in_specs=[
            pl.BlockSpec((tokens, part), lambda i: (0, i)),
            pl.BlockSpec((tokens, part), lambda i: (0, i)),
            pl.BlockSpec(act.shape, lambda i: (0, 0)),
            pl.BlockSpec(hid.shape, lambda i: (0, 0)),
        ]
        * len(sets),
        out_specs=[
            pair_spec,
            pl.BlockSpec((depth, units // depth, part), lambda i: (0, 0, i)),
        ],
        out_shape=[
            pltpu.HBM((depth, units2, width // depth), BF16),
            pltpu.HBM((depth, units // depth, width), BF16),
        ],
        compiler_params=pltpu.CompilerParams(vmem_limit_bytes=50 << 20),
        cost_estimate=pl.CostEstimate(
            flops=6 * tokens * width * units * len(sets),
            transcendentals=0,
            bytes_accessed=2 * (2 * tokens * width + 3 * units * tokens) * len(sets)
            + 6 * units * width,
        ),
        name="feed_weights",
    )(*[v for group in sets for v in group])


def reduce_last(first, first_y, second, second_x):
    first, second = add(first, first_y), add(second, second_x)
    return first[0], first[1], second[0], second[1]


def reduce_done(first, first_x, second, second_y):
    first = first.astype(F32) + first_x.astype(F32)
    second = second.astype(F32) + second_y.astype(F32)
    return jnp.concatenate([first, second], axis=-1)


LOG2E = 1.4426950408889634


def write_bias(query_ref, key_ref, bias_ref):
    query_code = query_ref[:, 0:1]
    query_pos = query_ref[:, 1:2]
    key_code = key_ref[0:1, :]
    key_pos = key_ref[1:2, :]
    key_valid = key_ref[2:3, :]
    allowed = (
        (query_code == key_code)
        & (key_pos <= query_pos)
        & ((key_valid == 1) | (key_pos == query_pos))
    )
    bias_ref[...] = jnp.where(allowed, 0.0, -1e30)


def forward_kernel(query_ref, key_ref, q_ref, k_ref, v_ref, out_ref, low_ref, bias_ref, *, scale):
    @pl.when(pl.program_id(0) == 0)
    def _():
        write_bias(query_ref, key_ref, bias_ref)

    scores = dot_nt(q_ref[...], k_ref[...])
    weights = jnp.exp2(scores * (scale * LOG2E) + bias_ref[...])
    totals = jnp.sum(weights, axis=-1, keepdims=True)
    unnorm = dot_nn(weights.astype(BF16), v_ref[...])
    attended = unnorm / totals
    out_ref[...] = attended
    low_ref[...] = attended.astype(BF16)


def backward_kernel(
    query_ref, key_ref, q_ref, k_ref, v_ref, att_ref, grad_ref, dq_ref, dk_ref, dv_ref, bias_ref, *, scale
):
    @pl.when(pl.program_id(0) == 0)
    def _():
        write_bias(query_ref, key_ref, bias_ref)

    q, k, v = q_ref[...], k_ref[...], v_ref[...]
    grad = grad_ref[...]
    scores = dot_nt(q, k)
    weights = jnp.exp2(scores * (scale * LOG2E) + bias_ref[...])
    totals = jnp.sum(weights, axis=-1, keepdims=True)
    grad_totals = -jnp.sum(grad * att_ref[...], axis=-1, keepdims=True) / totals
    grad_unnorm = (grad / totals).astype(BF16)
    grad_weights = dot_nt(grad_unnorm, v)
    grad_scores = (weights * (grad_weights + grad_totals)).astype(BF16)
    dq_ref[...] = (dot_nn(grad_scores, k) * scale).astype(BF16)
    dk_ref[...] = (dot_tn(grad_scores, q) * scale).astype(BF16)
    dv_ref[...] = dot_tn(weights.astype(BF16), grad_unnorm).astype(BF16)


def attention_specs(rows, keys):
    whole = lambda shape: pl.BlockSpec(shape, lambda h: (0, 0))
    head = lambda n, first=0: pl.BlockSpec((n, HEAD_DIM), lambda h: (0, first + h))
    return whole, head


def attend_forward(query_info, key_info, queries, pairs):
    rows, width = queries.shape
    count = pairs.shape[0]
    whole, head = attention_specs(rows, count)
    return pl.pallas_call(
        functools.partial(forward_kernel, scale=1.0 / math.sqrt(HEAD_DIM)),
        grid=(width // HEAD_DIM,),
        in_specs=[
            whole(query_info.shape),
            whole(key_info.shape),
            head(rows),
            head(count),
            head(count, width // HEAD_DIM),
        ],
        out_specs=[head(rows), head(rows)],
        out_shape=[
            jax.ShapeDtypeStruct((rows, width), F32),
            jax.ShapeDtypeStruct((rows, width), BF16),
        ],
        scratch_shapes=[pltpu.VMEM((rows, count), F32)],
        compiler_params=pltpu.CompilerParams(vmem_limit_bytes=40 << 20),
        cost_estimate=pl.CostEstimate(
            flops=4 * rows * count * width,
            transcendentals=rows * count * width // HEAD_DIM,
            bytes_accessed=2 * (2 * count + 4 * rows) * width,
        ),
        name="attend_forward",
    )(query_info, key_info, queries, pairs, pairs)


def attend_backward(query_info, key_info, queries, pairs, attended, grads):
    rows, width = queries.shape
    count = pairs.shape[0]
    whole, head = attention_specs(rows, count)
    return pl.pallas_call(
        functools.partial(backward_kernel, scale=1.0 / math.sqrt(HEAD_DIM)),
        grid=(width // HEAD_DIM,),
        in_specs=[
            whole(query_info.shape),
            whole(key_info.shape),
            head(rows),
            head(count),
            head(count, width // HEAD_DIM),
            head(rows),
            head(rows),
        ],
        out_specs=[head(rows), head(count), head(count)],
        out_shape=[
            jax.ShapeDtypeStruct((rows, width), BF16),
            jax.ShapeDtypeStruct((count, width), BF16),
            jax.ShapeDtypeStruct((count, width), BF16),
        ],
        scratch_shapes=[pltpu.VMEM((rows, count), F32)],
        compiler_params=pltpu.CompilerParams(vmem_limit_bytes=48 << 20),
        cost_estimate=pl.CostEstimate(
            flops=10 * rows * count * width,
            transcendentals=rows * count * width // HEAD_DIM,
            bytes_accessed=2 * (4 * count + 6 * rows) * width,
        ),
        name="attend_backward",
    )(query_info, key_info, queries, pairs, pairs, attended, grads)


def shards(
    inputs,
    kv_input,
    segment_ids,
    valid_mask,
    w_query,
    w_key,
    w_value,
    w_out,
    w_gate,
    w_up,
    w_down,
    gain_attn,
    gain_ffn,
    cotangent,
):
    rows, width = inputs.shape
    x, core, z, y = (lax.axis_index(name) for name in ALL)
    depth = lax.axis_size("z")
    devices = 4 * depth * 2
    dp, fsdp = x * 2 + core, z * 2 + y
    group_rows = rows * depth * 2
    seq_length = min(SEQ_LEN, group_rows)
    wide = w_query.shape[0]
    hidden = w_down.shape[0]

    small = jnp.concatenate(
        [gain_attn.astype(F32), gain_ffn.astype(F32), segment_ids.astype(F32), valid_mask.astype(F32)]
    )
    small = lax.all_to_all(
        jnp.broadcast_to(small[None], (devices, small.shape[0])), ALL, 0, 0, tiled=True
    )
    reach = min(-(-(seq_length // 2 - 1) // (2 * rows)), depth - 1)
    natural = 2 * wide % 128 == 0


    weights = jnp.concatenate([w_key, w_value, w_query, w_out], axis=1)
    weights = lax.all_gather(weights, ALL, axis=0, tiled=True)
    levels = [kv_input, shift(kv_input, "z", 1)]
    others = [swap(kv_input, "y")]
    cot_y = swap(cotangent, "y")

    def split_columns(w):
        return w.reshape(wide, 4, depth, 2, hidden).transpose(1, 3, 0, 2, 4)

    pair = jnp.stack([split_columns(w_gate), split_columns(w_up)], axis=2)
    pair = pair.reshape(8, 2 * wide, depth * hidden)
    levels[1], others[0], pair, cot_y = together(levels[1], others[0], pair, cot_y)

    others.append(swap(levels[1], "y"))
    for _ in range(reach - 1):
        levels.append(shift(levels[-1], "z", 1))
    for level in levels[2:-1]:
        others.append(swap(level, "y"))
    pair = lax.all_to_all(pair, GROUP, 0, 0, tiled=True)
    cot_pair = jnp.concatenate([cotangent, cot_y])
    pair, cot_pair, *held = together(pair, cot_pair, *others, *levels[1:])
    others, levels = held[: len(others)], [kv_input] + held[len(others) :]

    if len(others) < len(levels):
        others.append(swap(levels[-1], "y"))
    pair = pair.reshape(8, 2, wide, depth * hidden).transpose(1, 3, 0, 2)
    pair = settle(pair.reshape(2 * depth * hidden, 8 * wide))
    *held, pair, small = together(*levels, *others, pair, small)
    halo = join([held[i + j] for i in range(reach + 1) for j in (0, reach + 1)])
    halo_far, halo_near = columns(halo, 1, 3, dp), columns(halo, 0, 2, dp)
    full_gain_attn = small[:, :wide].reshape(-1)
    full_gain_ffn = small[:, wide : 2 * wide].reshape(-1)
    ids_all = lax.dynamic_slice_in_dim(small, dp * depth * 2, depth * 2, 0)[:, 2 * wide :]
    ids_all = ids_all.astype(jnp.int32)
    block_ids = []
    for level in range(reach + 1):
        for other in range(2):
            block_ids.append(2 * (z - level) + (y ^ other))
    key_pos, key_seg, key_valid = [], [], []
    for block in block_ids:
        here = pick(ids_all, jnp.maximum(block, 0), 0)
        key_seg.append(here[:rows])
        key_valid.append(here[rows:])
        key_pos.append(block * rows + jnp.arange(rows, dtype=jnp.int32))
    key_pos, key_seg, key_valid = (jnp.concatenate(v) for v in (key_pos, key_seg, key_valid))
    query_pos = fsdp * rows + jnp.arange(rows, dtype=jnp.int32)
    code = lambda seg, pos: seg * 4096 + pos // seq_length
    zeros = jnp.zeros_like(key_pos)
    key_info = jnp.stack([code(key_seg, key_pos), key_pos, key_valid] + [zeros] * 5)
    zeros = jnp.zeros_like(query_pos)
    query_info = jnp.stack([code(segment_ids, query_pos), query_pos] + [zeros] * 6, axis=1)
    stream = inputs.astype(F32)
    squares_in = jnp.sum(stream * stream, axis=-1, keepdims=True)
    factor_one = lax.rsqrt(squares_in / width + EPSILON)
    unit_one = stream * factor_one
    normed1 = (unit_one * full_gain_attn).astype(BF16)
    normed1_far, normed1_near = columns(normed1, 1, 3, dp), columns(normed1, 0, 2, dp)
    (
        pair, weights, cot_pair, down, halo, halo_far, halo_near, full_gain_ffn, normed1, normed1_far,
        normed1_near, query_info, key_info,
    ) = together(
        pair, weights, cot_pair, w_down, halo, halo_far, halo_near, full_gain_ffn, normed1,
        normed1_far, normed1_near, query_info, key_info,
    )

    pair = lax.all_gather(pair, "z", axis=0, tiled=False)
    cot_x = swap(cot_pair, "x")
    pairs = project([halo], weights, 0, 2, BF16)
    cot_x, pairs = together(cot_x, pairs)
    queries = project([normed1], weights, 2, 1, BF16)
    attended_f, attended = attend_forward(query_info, key_info, queries, pairs)
    middle = stream + project([attended], weights, 3, 1, F32)
    squares_mid = jnp.sum(middle * middle, axis=-1, keepdims=True)
    factor_two = lax.rsqrt(squares_mid / width + EPSILON)
    unit_two = middle * factor_two
    normed2 = (unit_two * full_gain_ffn).astype(BF16)
    if not natural:
        normed2 = normed2.reshape(rows, 4, depth, 2 * wide).swapaxes(1, 2).reshape(rows, width)
    half = width // 2
    first, second, cot_x = together(normed2[:, :half], normed2[:, half:], cot_x)
    cot_near = jnp.concatenate([cot_pair, cot_x])
    cot_far = swap(cot_near, "core")

    first_x, second_y = swap(first, "x"), swap(second, "y")
    first_x, second_y, cot_near, cot_far, pair, down = together(
        first_x, second_y, cot_near, cot_far, pair, down
    )
    part_down = lax.all_gather(down, "z", axis=0, tiled=False)
    first, second = jnp.stack([first, first_x]), jnp.stack([second, second_y])
    first_y, second_x = swap(first, "y"), swap(second, "x")
    attended_far, attended_near = columns(attended, 1, 3, dp), columns(attended, 0, 2, dp)
    first_y, second_x, attended_far, attended_near = together(
        first_y, second_x, attended_far, attended_near
    )
    first = jnp.stack([first, first_y], axis=1)
    second = jnp.stack([second, second_x])
    x_near = jnp.concatenate([first, second], axis=-1).reshape(4 * rows, width)
    x_far = swap(x_near, "core")
    feeds = pair
    part_down = part_down.reshape(depth * hidden, width)

    out_far, grad_far, act_far, hid_far = feed(x_far, cot_far, feeds, part_down, natural)
    got = swap(grad_far, "core")
    out_near, act_near, hid_near, first, first_away, second, second_away = feed(
        x_near, cot_near, feeds, part_down, natural, got
    )
    out_got = swap(out_far, "core")
    first_y, second_x = swap(first_away, "y"), swap(second_away, "x")
    grad_pair, grad_down = feed_weights(
        [(x_near, cot_near, act_near, hid_near), (x_far, cot_far, act_far, hid_far)], depth, natural
    )
    first, first_away, second, second_away = reduce_last(first, first_y, second, second_x)
    first, first_away, second, second_away, grad_pair, grad_down, out_near, out_got = together(
        first, first_away, second, second_away, grad_pair, grad_down, out_near, out_got
    )
    grad_pair = lax.psum_scatter(grad_pair, "z", scatter_dimension=0, tiled=True)
    grad_down = lax.psum_scatter(grad_down, "z", scatter_dimension=0, tiled=True)
    first_x, second_y = swap(first_away, "x"), swap(second_away, "y")
    grad_normed2 = reduce_done(first, first_x, second, second_y)
    if not natural:
        grad_normed2 = grad_normed2.reshape(rows, depth, 4, 2 * wide).swapaxes(1, 2)
        grad_normed2 = grad_normed2.reshape(rows, width)

    part_gain_ffn = jnp.sum(grad_normed2 * unit_two, axis=0)
    inner = grad_normed2 * full_gain_ffn
    grad_middle = cotangent.astype(F32) + factor_two * (
        inner - unit_two * jnp.mean(inner * unit_two, axis=-1, keepdims=True)
    )
    grad_branch = grad_middle.astype(BF16)
    far_out = weight_grad(attended_far, grad_branch)
    far_out, grad_branch, grad_middle = together(far_out, grad_branch, grad_middle)
    got_out = swap(far_out, "core")
    grad_attended = project_back([grad_branch], weights, [3], F32)
    out_home, out_away = weight_grad(attended_near, grad_branch, got_out, 2)
    out_home, out_away, grad_attended = together(out_home, out_away, grad_attended)

    out_x = swap(out_away, "x")
    grad_queries, grad_keys, grad_values = attend_backward(
        query_info, key_info, queries, pairs, attended_f, grad_attended
    )
    far_key = weight_grad(halo_far, grad_keys)
    out_x, far_key, grad_keys, grad_values, grad_queries = together(
        out_x, far_key, grad_keys, grad_values, grad_queries
    )

    got_key = swap(far_key, "core")
    far_value = weight_grad(halo_far, grad_values)
    got_key, far_value, grad_keys, grad_values, grad_queries, grad_pair = together(
        got_key, far_value, grad_keys, grad_values, grad_queries, grad_pair
    )

    got_value = swap(far_value, "core")
    key_home, key_away = weight_grad(halo_near, grad_keys, got_key, 2)
    got_value, key_home, key_away, grad_keys, grad_values, grad_queries = together(
        got_value, key_home, key_away, grad_keys, grad_values, grad_queries
    )

    value_near = weight_grad(halo_near, grad_values, got_value)
    value_near, key_away, grad_keys, grad_values, grad_queries = together(
        value_near, key_away, grad_keys, grad_values, grad_queries
    )

    key_x = swap(key_away, "x")
    value_away, value_home = split_y(value_near.reshape(2, depth, 2, wide, width))
    value_y = swap(value_away, "y")
    grad_pair = settle(settle(grad_pair.reshape(2 * depth * hidden, 8 * wide)).T)
    grad_pair = grad_pair.reshape(8, wide, 2 * depth * hidden)
    grad_pair = lax.all_to_all(grad_pair, GROUP, 0, 0, tiled=True)
    halves = [grad_keys, grad_values]
    back = project_back(halves, weights, [0, 1], BF16, reach, 2 * rows)
    back = shift(back, "z", -1)
    grad_halo = project_back(halves, weights, [0, 1], BF16, 0, reach * 2 * rows)
    got_query = swap(weight_grad(normed1_far, grad_queries), "core")
    query_home, query_away = weight_grad(normed1_near, grad_queries, got_query, 2)
    key_x, value_y, query_home, query_away, grad_halo, back, grad_queries, *held = together(
        key_x, value_y, query_home, query_away, grad_halo, back, grad_queries, grad_pair, out_near, out_got,
        grad_down, out_home, out_x,
    )
    grad_pair, out_near, out_got, grad_down, out_home, out_x = held
    out_away, out_home = split_y(by_owner(add(out_home, out_x)))
    share_down = grad_down.reshape(hidden, width).astype(F32)

    key_away, key_home = split_y(by_owner(add(key_home, key_x)))
    query_x, key_y, out_y = swap(query_away, "x"), swap(key_away, "y"), swap(out_away, "y")
    for level in reversed(range(1, reach)):
        at = level * 2 * rows
        back = shift(add(grad_halo[at : at + 2 * rows], back), "z", -1)
    grad_normed1 = project_back([grad_queries], weights, [2], F32)
    value_home = add(value_home, value_y)
    sums = add(out_near, out_got).reshape(2, 2, rows, width)
    sums = sums[:, 0, :, :half], sums[:, 1, :, :half], sums[0, :, :, half:], sums[1, :, :, half:]
    query_x, key_y, out_y, back, grad_normed1, grad_pair, value_home, *sums = together(
        query_x, key_y, out_y, back, grad_normed1, grad_pair, value_home, *sums
    )

    shares_first = jnp.concatenate([add(key_home, key_y), add(out_home, out_y)], axis=1)
    shares_first = lax.psum_scatter(shares_first, "z", scatter_dimension=0, tiled=True)
    query_away, query_home = split_y(by_owner(add(query_home, query_x)))
    query_y, value_x = swap(query_away, "y"), swap(value_home[1], "x")
    sum_y, sum_x = swap(sums[1], "y"), swap(sums[3], "x")
    back = add(grad_halo[: 2 * rows], back)
    grad_pair = grad_pair.reshape(4, 2, wide, 2, depth, hidden).transpose(3, 2, 0, 4, 1, 5)
    grad_pair = grad_pair.reshape(2, wide, devices * hidden).astype(F32)
    part_gain_attn = jnp.sum(grad_normed1 * unit_one, axis=0)
    inner = grad_normed1 * full_gain_attn
    grad_inputs = grad_middle + factor_one * (
        inner - unit_one * jnp.mean(inner * unit_one, axis=-1, keepdims=True)
    )
    query_y, value_x, back, sum_y, sum_x, share_gate, share_up, grad_inputs = together(
        query_y, value_x, back, sum_y, sum_x, grad_pair[0], grad_pair[1], grad_inputs
    )

    shares = jnp.concatenate([add(value_home[0], value_x), add(query_home, query_y)], axis=1)
    shares = lax.psum_scatter(shares, "z", scatter_dimension=0, tiled=True)
    sums = reduce_last(sums[0], sum_y, sums[2], sum_x)
    sum_x, sum_y, back_y = swap(sums[1], "x"), swap(sums[3], "y"), swap(back[rows:], "y")
    sum_x, sum_y = together(sum_x, sum_y)
    grad_kv_input = back[:rows].astype(F32) + back_y.astype(F32)
    result = middle + reduce_done(sums[0], sum_x, sums[2], sum_y)
    valid = valid_mask.astype(F32)
    squares_out = jnp.sum(result * result, axis=-1)
    sums = jnp.stack(
        [
            jnp.sum(valid * squares_in[:, 0]),
            jnp.sum(valid * squares_mid[:, 0]),
            jnp.sum(valid * squares_out),
            jnp.sum(valid),
        ]
    )
    tiny = jnp.concatenate(
        [
            part_gain_attn.reshape(devices, wide),
            part_gain_ffn.reshape(devices, wide),
            jnp.broadcast_to(sums[None], (devices, 4)),
        ],
        axis=1,
    )
    tiny = lax.all_to_all(tiny, ALL, 0, 0, tiled=True)
    share_key, share_out = shares_first[0, :wide].astype(F32), shares_first[0, wide:].astype(F32)
    share_value, share_query = shares[0, :wide].astype(F32), shares[0, wide:].astype(F32)

    tiny = jnp.sum(tiny, axis=0)
    divisor = tiny[2 * wide + 3] * width
    rms_in = jnp.sqrt(tiny[2 * wide] / divisor)
    rms_mid = jnp.sqrt(tiny[2 * wide + 1] / divisor)
    rms_out = jnp.sqrt(tiny[2 * wide + 2] / divisor)
    return (
        result.astype(BF16),
        grad_inputs,
        grad_kv_input,
        share_query,
        share_key,
        share_value,
        share_out,
        share_gate,
        share_up,
        share_down,
        tiny[:wide],
        tiny[wide : 2 * wide],
        rms_in,
        rms_mid,
        rms_out,
    )


def solution(mesh):
    inner = Mesh(
        mesh.devices.reshape(2, mesh.shape["dp"] // 2, mesh.shape["fsdp"] // 2, 2), ALL
    )
    rows, flat = P(ALL, None), P(ALL)
    return jax.shard_map(
        shards,
        mesh=inner,
        in_specs=(rows, rows, flat, flat) + (rows,) * 7 + (flat, flat, rows),
        out_specs=(rows,) * 10 + (flat, flat, P(), P(), P()),
        check_vma=False,
    )
```
